256 devices in a mesh: mem: 4 (over y_hi, core), reg: 64 (over y_lo, x, z).
Axes of the slice: x: 4, y: 4 (y_hi: 2, y_lo: 2; y = y_hi * 2 + y_lo), z: 8, core: 2. Of those that a mesh axis runs over, the one named last changes fastest.
Arguments:
- prior_samples: bfloat16 [256, 512, 512], P('mem', 'reg'), may hold values from -6 to 6
- measured_sample_anomalies: bfloat16 [16384, 128, 256], P(('mem', 'reg')), may hold values from -4 to 4
- reciprocal_noise_spread: float32 [16384, 128], P(('mem', 'reg')), may hold values from 0.3 to 3
- measured_departure: float32 [16384, 128], P(('mem', 'reg')), may hold values from -6 to 6
- measurement_tally: int32 [16384], P(('mem', 'reg')), may hold values from 32 to 128
- group_destination_zone: int32 [16384, 1], P(('mem', 'reg')), may hold values from 0 to 63; in each aligned block of 64 rows (0 to 63, 64 to 127, ...) at most 2 rows name the same one
- group_nearby_tile: int32 [16384], P(('mem', 'reg')), may hold values from 0 to 7
Outputs:
- analysis: bfloat16 [256, 512, 512], P('mem', 'reg')
The draws below stay inside these ranges and needn't reach their ends.
Inputs may be any that keep to these rules, and one draw needn't show every extreme that they name: `measurement_tally`: valid observations of a block stand in its first rows. `group_destination_zone`: at most 2 of the blocks of one device name the same region; in every draw some device has exactly 2 blocks naming one region.
All inputs are finite; a program needn't handle non-finite values.
Results may differ from the reference program's by a relative error of at most 0.0069.
Values may be sent and summed in bfloat16 or wider, within the bound.
No kernel may reach another device: no remote copies, remote signals or barrier semaphores. Data moves between devices by JAX's collectives and lax.ppermute only.
A program may use at most 128 MiB of HBM per device.

```python
import math
import jax
import jax.numpy as jnp
import numpy as np
from jax import lax

SAMPLE_NUMBER = 256
TILE_SIZE = 512
OB = 128
BLK_DEV = 64
ITERS = 5
CAP = 2
PATCH_REG = 8
TILE_NUMBER = 512
NBLK = 16384
N_REG = 64


def plant(result, own_key, low, high):
    extent = result.shape
    spot = [jax.random.randint(jax.random.fold_in(own_key, axis), (), 0, extent[axis]) for axis in range(len(extent))]
    result = result.at[tuple(spot)].set(low)
    longest = extent.index(max(extent))
    spot[longest] = (spot[longest] + 1) % extent[longest]
    return result.at[tuple(spot)].set(high)


def shard_levels(rng, extent, shards, least, high):
    level = 1.0
    for axis_at, parts in shards:
        heights = jax.random.uniform(jax.random.fold_in(jax.random.fold_in(rng, 6), axis_at), (parts,), jnp.float32, least / len(shards), high / len(shards))
        level = level * jnp.repeat(jnp.exp(heights), extent[axis_at] // parts).reshape((-1,) + (1,) * (len(extent) - 1 - axis_at))
    return level


def routed_block(rng, own, number, rows, count, top, reach, skew):
    sequence = jax.random.permutation(rng, count)
    heavy_load, usual = load_shares(count, rows * top, reach, skew, True), load_shares(count, rows * top, reach, skew, False)
    places = jnp.arange(count)

    def named(tallies, turn):
        used = int((tallies > 0).sum())
        fixed = max(1, used // 4)
        passed = fixed + (places - fixed + turn * (used - fixed)) % max(1, count - fixed)
        return jnp.zeros((count,), jnp.int32).at[sequence[jnp.where(places < fixed, places, passed)]].set(jnp.asarray(tallies, jnp.int32))

    tallies = jnp.where(number % 4 == 0, named(heavy_load, number // 4), named(usual, number - number // 4 - 1))
    mixed = jax.random.permutation(jax.random.fold_in(own, 3), count)
    donor, taker = mixed[0:count // 2 * 2:2], mixed[1:count // 2 * 2:2]
    room = jnp.minimum(tallies[donor] - 1, reach - tallies[taker]) // 2
    room = jnp.where((donor == sequence[0]) | (taker == sequence[0]) | (tallies[taker] == 0), 0, jnp.maximum(room, 0))
    passed = jax.random.randint(jax.random.fold_in(own, 4), (count // 2,), 0, 1 << 20) % (room + 1)
    tallies = tallies.at[donor].add(-passed).at[taker].add(passed)
    labels = jnp.searchsorted(jnp.cumsum(tallies), jnp.arange(rows * top), side="right").astype(jnp.int32)
    grid = labels.reshape(top, rows).T
    grid = grid[jax.random.permutation(jax.random.fold_in(own, 1), rows)]
    turn = jax.random.randint(jax.random.fold_in(own, 2), (rows, 1), 0, top)
    return jnp.take_along_axis(grid, (jnp.arange(top)[None, :] + turn) % top, axis=1)


def load_shares(number_of, total, limit, skew, full):
    loads = [(1 << 20) // math.isqrt(grade ** skew) + 1 for grade in range(1, number_of + 1)]
    largest = limit if full else min(limit, max(-(-total // number_of), total * loads[0] // sum(loads)))
    least = 1 if total - largest >= number_of - 1 else 0
    counts, rest = [largest] + [least] * (number_of - 1), total - largest - least * (number_of - 1)
    while rest > 0:
        movable = [i for i in range(1, number_of) if counts[i] < largest] or [i for i in range(1, number_of) if counts[i] < limit]
        pool, budget = sum([loads[i] for i in movable]), rest
        for i in movable:
            addition = min(limit - counts[i], max(1, budget * loads[i] // pool), rest)
            counts[i] = counts[i] + addition
            rest = rest - addition
    return np.array(counts)


def bell_draw(rng, shape, spread, bound, shards=(), kind=jnp.bfloat16):
    result = spread * jax.random.normal(rng, shape, jnp.float32)
    if shards:
        result = result * shard_levels(rng, shape, shards, -0.22, 0.18)
    return jnp.clip(result, -bound, bound).astype(kind)


def setup_inputs(seed: int = 0) -> dict:
    splits = jax.random.split(jax.random.key(seed), 8)
    prior_samples = bell_draw(splits[0], (SAMPLE_NUMBER, TILE_NUMBER, TILE_SIZE), 1.0, 6.0, ((0, 4), (1, 64)))
    measured_sample_anomalies = bell_draw(splits[1], (NBLK, OB, SAMPLE_NUMBER), 0.6, 4.0, ((0, 256),))
    reciprocal_noise_spread = jnp.clip(jnp.exp(math.log(3.0) - 2.3025851 * jax.random.uniform(splits[2], (NBLK, OB), jnp.float32) ** shard_levels(splits[2], (NBLK, OB), ((0, 256),), -0.2, 0.2)), 0.3, 3.0)
    measured_departure = bell_draw(splits[3], (NBLK, OB), 1.0, 6.0, ((0, 256),), jnp.float32)
    measurement_tally = plant(jax.random.randint(splits[4], (NBLK,), OB // 4, OB + 1), jax.random.fold_in(splits[4], 1), OB // 4, OB).astype(jnp.int32)
    group_destination_zone_keys = jax.random.split(jax.random.fold_in(splits[5], 1), NBLK // BLK_DEV)
    group_destination_zone_turns = jax.random.permutation(jax.random.fold_in(splits[5], 3), NBLK // BLK_DEV)
    group_destination_zone = jax.vmap(lambda own, number: routed_block(jax.random.fold_in(splits[5], 2), own, number, BLK_DEV, N_REG, 1, CAP, 2))(group_destination_zone_keys, group_destination_zone_turns).reshape((NBLK, 1))
    group_nearby_tile = plant(jax.random.randint(splits[6], (NBLK,), 0, PATCH_REG), jax.random.fold_in(splits[6], 1), 0, PATCH_REG - 1).astype(jnp.int32)
    return {"prior_samples": prior_samples, "measured_sample_anomalies": measured_sample_anomalies, "reciprocal_noise_spread": reciprocal_noise_spread, "measured_departure": measured_departure, "measurement_tally": measurement_tally, "group_destination_zone": group_destination_zone, "group_nearby_tile": group_nearby_tile}


def matmul_high(left, right):
    return jnp.matmul(left, right, precision=lax.Precision.HIGHEST)

def weight_matrices(gram_part, drive_part):
    identity = jnp.eye(SAMPLE_NUMBER, dtype=jnp.float32)
    gram_full = gram_part + (SAMPLE_NUMBER - 1.0) * identity
    frob_scale = jnp.sqrt(lax.optimization_barrier(jnp.sum(gram_full * gram_full, axis=(1, 2))))[:, None, None]
    root_iter = gram_full / frob_scale
    inverse_iter = jnp.broadcast_to(identity, gram_full.shape)
    for sweep in range(ITERS):
        newton_step = 1.5 * identity - 0.5 * matmul_high(inverse_iter, root_iter)
        root_iter = matmul_high(root_iter, newton_step)
        inverse_iter = matmul_high(newton_step, inverse_iter)
    inv_root = inverse_iter / jnp.sqrt(frob_scale)
    mean_weight = matmul_high(inv_root, matmul_high(inv_root, drive_part[:, :, None]))
    return (math.sqrt(SAMPLE_NUMBER - 1.0) * inv_root + mean_weight).astype(jnp.bfloat16)

def reference(prior_samples, measured_sample_anomalies, reciprocal_noise_spread, measured_departure, measurement_tally, group_destination_zone, group_nearby_tile):
    is_valid = lax.broadcasted_iota(jnp.int32, reciprocal_noise_spread.shape, 1) < measurement_tally[:, None]
    row_weight = jnp.where(is_valid, reciprocal_noise_spread, jnp.zeros_like(reciprocal_noise_spread))
    scaled = (measured_sample_anomalies * row_weight[:, :, None]).astype(jnp.bfloat16)
    weighted = (measured_departure * row_weight).astype(jnp.bfloat16)
    patch_index = (group_destination_zone[:, 0] * PATCH_REG + group_nearby_tile).astype(jnp.int32)
    groups = NBLK // BLK_DEV

    def accumulate(totals, block_item):
        rows_block, obs_block, patch_block = block_item
        rows_wide = rows_block.astype(jnp.float32)
        block_grams = jnp.einsum('gok,gol->gkl', rows_wide, rows_wide, precision=lax.Precision.HIGHEST)
        drives = jnp.einsum('gok,go->gk', rows_wide, obs_block.astype(jnp.float32), precision=lax.Precision.HIGHEST)
        return ((totals[0].at[patch_block].add(block_grams), totals[1].at[patch_block].add(drives)), None)
    start_totals = (jnp.zeros((TILE_NUMBER, SAMPLE_NUMBER, SAMPLE_NUMBER), jnp.float32), jnp.zeros((TILE_NUMBER, SAMPLE_NUMBER), jnp.float32))
    (gram_sum, drive_sum), unused = lax.scan(accumulate, start_totals, (scaled.reshape(groups, BLK_DEV, OB, SAMPLE_NUMBER), weighted.reshape(groups, BLK_DEV, OB), patch_index.reshape(groups, BLK_DEV)))
    weights = weight_matrices(gram_sum, drive_sum)
    sample_average_field = lax.optimization_barrier(jnp.mean(prior_samples.astype(jnp.float32), axis=0))
    sample_deviation_field = (prior_samples - sample_average_field).astype(jnp.bfloat16)
    update = jnp.einsum('jpx,pjk->kpx', sample_deviation_field.astype(jnp.float32), weights.astype(jnp.float32), precision=lax.Precision.HIGHEST)
    return (sample_average_field[None] + update).astype(jnp.bfloat16)
```

```python
import functools
import math

import jax
import jax.numpy as jnp
from jax import lax
from jax.experimental import pallas as pl
from jax.experimental.pallas import tpu as pltpu
from jax.sharding import Mesh
from jax.sharding import PartitionSpec as P

SAMPLE_NUMBER = 256
OB = 128
CAP = 2
PATCH_REG = 8
ITERS = 5
META = 16
ROWS = CAP * OB + META
HALF = SAMPLE_NUMBER // 2
MEMBERS = SAMPLE_NUMBER // 4
PACK = 2 * HALF + 16
GROUP = ("mem", "ylo", "x", "zp")
STEP = 8
TAGS = 16


def prep_kernel(
    ways, zone_smem, tally_smem, tile_smem, anom_ref, spread_ref, depart_ref, out_ref, anom_buf,
    meta_wide, counts, sems
):
    blocks = anom_ref.shape[0]
    regions = out_ref.shape[0]
    zq_ways, plane_ways, zp_ways = ways

    def load(g):
        part = pl.ds(g * STEP, STEP)
        return pltpu.make_async_copy(anom_ref.at[part], anom_buf.at[part], sems.at[g])

    for g in range(blocks // STEP):
        load(g).start()

    @pl.loop(0, regions)
    def _(r):
        counts[r] = 0

    meta_wide[...] = jnp.zeros_like(meta_wide)
    row = lax.broadcasted_iota(jnp.int32, (OB, 1), 0)
    lane = lax.broadcasted_iota(jnp.int32, (1, OB), 1)

    @pl.loop(0, blocks // STEP)
    def _(g):
        part = pl.ds(pl.multiple_of(g * STEP, STEP), STEP)
        spread, depart = spread_ref[part, :], depart_ref[part, :]
        spread_t = spread.T
        load(g).wait()
        for j in range(STEP):
            b = g * STEP + j
            region = zone_smem[b]
            rank = counts[region]
            counts[region] = rank + 1
            rest = region // zp_ways
            place = (rest % zq_ways * plane_ways + rest // zq_ways) * zp_ways + region % zp_ways

            weight = jnp.where(row < tally_smem[b], spread_t[:, j : j + 1], 0.0)
            scaled = anom_buf[b].astype(jnp.float32) * weight
            start = pl.multiple_of(rank * OB, OB)
            out_ref[place, pl.ds(start, OB), :] = scaled.astype(jnp.bfloat16)

            kept = jnp.where(lane < tally_smem[b], spread[j : j + 1], 0.0)
            tag = jnp.full((1, OB), tile_smem[b] + 1, jnp.int32).astype(jnp.float32)
            content = jnp.concatenate([depart[j : j + 1] * kept, tag], axis=1)
            meta_wide[place, pl.ds(rank, 1), :] = content

    out_ref[:, CAP * OB :, :] = meta_wide[...].astype(jnp.bfloat16)


def build_messages(anomalies, spread, departure, tally, tile, zone, ways):
    blocks = anomalies.shape[0]
    regions = math.prod(ways)
    scalars = pl.BlockSpec(memory_space=pltpu.SMEM)
    vectors = pl.BlockSpec(memory_space=pltpu.VMEM)
    return pl.pallas_call(
        functools.partial(prep_kernel, ways),
        out_shape=jax.ShapeDtypeStruct((regions, ROWS, SAMPLE_NUMBER), jnp.bfloat16),
        in_specs=[scalars] * 3 + [pl.BlockSpec(memory_space=pl.ANY)] + [vectors] * 2,
        out_specs=vectors,
        scratch_shapes=[
            pltpu.VMEM((blocks, OB, SAMPLE_NUMBER), jnp.bfloat16),
            pltpu.VMEM((regions, META, SAMPLE_NUMBER), jnp.float32),
            pltpu.SMEM((regions,), jnp.int32),
            pltpu.SemaphoreType.DMA((blocks // STEP,)),
        ],
        compiler_params=pltpu.CompilerParams(vmem_limit_bytes=24 << 20),
        cost_estimate=pl.CostEstimate(flops=0, bytes_accessed=1 << 23, transcendentals=0),
        name="build_messages",
    )(zone, tally, tile, anomalies, spread, departure)


def high_low(row):
    high = row.astype(jnp.bfloat16)
    return high, (row - high.astype(jnp.float32)).astype(jnp.bfloat16)


def gram_kernel(tag_ref, rows_ref, *refs):
    outs, (upper, corner, tag_vmem, tag_smem, tag_sem) = refs[:4], refs[4:]
    step, zq = pl.program_id(0), lax.axis_index("zq")
    sources = rows_ref.shape[0]

    @pl.when(step == 0)
    def _():
        weight = lax.broadcasted_iota(jnp.int32, tag_ref.shape, 1)
        weight = jnp.where(weight == 0, 1.0, jnp.where(weight == 1, TAGS, 0.0))
        codes = jnp.sum(tag_ref[...].astype(jnp.float32) * weight, axis=1)
        tag_vmem[...] = codes.astype(jnp.int32)
        tag_copy = pltpu.make_async_copy(tag_vmem, tag_smem, tag_sem)
        tag_copy.start()
        upper[...] = jnp.zeros_like(upper)
        corner[...] = jnp.zeros_like(corner)
        tag_copy.wait()

    place = lax.broadcasted_iota(jnp.int32, (META, OB), 0)
    for s in range(sources):
        meta = rows_ref[s, CAP * OB : ROWS, :OB].astype(jnp.float32)
        for i in range(CAP):
            code = tag_smem[step * sources + s, 0]
            tag = (code // TAGS if i else code % TAGS) - 1
            turned = (tag // 2 - zq + 4) % 4 * 2 + tag % 2
            tag = jnp.where(tag >= 0, turned, PATCH_REG)
            block = rows_ref[s, i * OB : (i + 1) * OB, :]
            flipped = block.T
            innovation = jnp.where(place == i, meta, 0.0).astype(jnp.bfloat16)
            left = jnp.concatenate([flipped[:HALF], innovation], axis=0)
            upper[tag] += jnp.dot(left, block, preferred_element_type=jnp.float32)
            corner[tag] += jnp.dot(
                flipped[HALF:], block[:, HALF:], preferred_element_type=jnp.float32
            )

    @pl.when(step == pl.num_programs(0) - 1)
    def _():
        row = lax.broadcasted_iota(jnp.int32, (HALF, HALF), 0)
        col = lax.broadcasted_iota(jnp.int32, (HALF, HALF), 1)
        for p in range(PATCH_REG):
            first, last = upper[p, :HALF, :HALF], corner[p]
            mixed = jnp.where(row >= col, first, last)
            diagonal = jnp.sum(jnp.where(row == col, last, 0.0), axis=0, keepdims=True)
            drive = jnp.sum(upper[p, HALF:, :], axis=0, keepdims=True)
            extra = jnp.concatenate([diagonal, drive[:, :HALF], drive[:, HALF:]], axis=0)
            high, low = high_low(extra)
            tail = jnp.concatenate(
                [
                    high.astype(jnp.float32),
                    low.astype(jnp.float32),
                    jnp.zeros((PACK - 2 * HALF - 6, HALF), jnp.float32),
                ],
                axis=0,
            )
            out = outs[p // 2]
            out[p % 2, :HALF, :] = upper[p, :HALF, HALF:].astype(jnp.bfloat16)
            out[p % 2, HALF : 2 * HALF, :] = mixed.astype(jnp.bfloat16)
            out[p % 2, 2 * HALF :, :] = tail.astype(jnp.bfloat16)


def partial_grams(messages):
    regions = messages.shape[0]
    sources = min(8, regions)
    piece = jax.ShapeDtypeStruct((2, PACK, HALF), jnp.bfloat16)
    return pl.pallas_call(
        gram_kernel,
        out_shape=[piece] * 4,
        grid_spec=pl.GridSpec(
            grid=(regions // sources,),
            in_specs=[
                pl.BlockSpec((regions, META, OB), lambda i: (0, CAP * OB // META, 1)),
                pl.BlockSpec((sources, ROWS, SAMPLE_NUMBER), lambda i: (i, 0, 0)),
            ],
            out_specs=[pl.BlockSpec((2, PACK, HALF), lambda i: (0, 0, 0))] * 4,
            scratch_shapes=[
                pltpu.VMEM((PATCH_REG + 1, HALF + META, SAMPLE_NUMBER), jnp.float32),
                pltpu.VMEM((PATCH_REG + 1, HALF, HALF), jnp.float32),
                pltpu.VMEM((regions, OB), jnp.int32),
                pltpu.SMEM((regions, OB), jnp.int32),
                pltpu.SemaphoreType.DMA,
            ],
        ),
        compiler_params=pltpu.CompilerParams(vmem_limit_bytes=12 << 20),
        cost_estimate=pl.CostEstimate(flops=1 << 31, bytes_accessed=1 << 23, transcendentals=0),
        name="partial_grams",
    )(messages, messages)


def split(a):
    high = a.astype(jnp.bfloat16)
    return high, (a - high.astype(jnp.float32)).astype(jnp.bfloat16)


def product(a, b):
    dot = functools.partial(jnp.dot, preferred_element_type=jnp.float32)
    return dot(a[0], b[0]) + (dot(a[0], b[1]) + dot(a[1], b[0]))


def newton_kernel(a_ref, b_ref, c_ref, d_ref, *refs):
    zq = lax.axis_index("zq")
    outs, (gram_ref, weight_ref) = refs[:4], refs[4:]
    row = lax.broadcasted_iota(jnp.int32, (HALF, HALF), 0)
    col = lax.broadcasted_iota(jnp.int32, (HALF, HALF), 1)
    row_full = lax.broadcasted_iota(jnp.int32, (SAMPLE_NUMBER, SAMPLE_NUMBER), 0)
    col_full = lax.broadcasted_iota(jnp.int32, (SAMPLE_NUMBER, SAMPLE_NUMBER), 1)
    identity = jnp.where(row_full == col_full, 1.0, 0.0)
    for p in range(2):
        total = sum(ref[p].astype(jnp.float32) for ref in (a_ref, b_ref, c_ref, d_ref))
        cross, mixed, tail = total[:HALF], total[HALF : 2 * HALF], total[2 * HALF :]
        extra = tail[0:3] + tail[3:6]
        turned = mixed.T
        gram_ref[p, :HALF, :HALF] = jnp.where(row >= col, mixed, turned)
        gram_ref[p, :HALF, HALF:] = cross
        gram_ref[p, HALF:, :HALF] = cross.T
        gram_ref[p, HALF:, HALF:] = jnp.where(
            row == col, extra[0:1], jnp.where(row < col, mixed, turned)
        )
        drive = jnp.concatenate([extra[1:2], extra[2:3]], axis=1)
        gram = gram_ref[p] + (SAMPLE_NUMBER - 1.0) * identity
        squares = jnp.sum(jnp.sum(gram * gram, axis=0, keepdims=True), axis=1, keepdims=True)
        frob = jnp.sqrt(squares)
        root = gram / frob
        inverse = step = 1.5 * identity - 0.5 * root
        for sweep in range(1, ITERS):
            step_parts = split(step)
            root = product(split(root), step_parts)
            inverse_parts = split(inverse)
            step = 1.5 * identity - 0.5 * product(inverse_parts, split(root))
            inverse = product(split(step), inverse_parts)
        inv_root = inverse / jnp.sqrt(frob)
        once = jnp.sum(inv_root * drive, axis=1, keepdims=True)
        mean_weight = jnp.sum(inv_root * once, axis=0, keepdims=True)
        weight_ref[...] = math.sqrt(SAMPLE_NUMBER - 1.0) * inv_root + mean_weight
        for e in range(4):
            goal = (zq + e) % 4
            part = weight_ref[pl.ds(pl.multiple_of(goal * MEMBERS, MEMBERS), MEMBERS), :]
            low, high = part[:, :HALF], part[:, HALF:]
            low, high = jnp.where(goal >= 2, high, low), jnp.where(goal >= 2, low, high)
            for i, side in enumerate((low, high)):
                side = jnp.where(goal % 2 == 1, pltpu.roll(side, MEMBERS, 1), side)
                outs[e][p, :, i * HALF : (i + 1) * HALF] = side.astype(jnp.bfloat16)


def flipped_weights(pieces):
    piece = jax.ShapeDtypeStruct((2, MEMBERS, SAMPLE_NUMBER), jnp.bfloat16)
    return pl.pallas_call(
        newton_kernel,
        out_shape=[piece] * 4,
        scratch_shapes=[
            pltpu.VMEM((2, SAMPLE_NUMBER, SAMPLE_NUMBER), jnp.float32),
            pltpu.VMEM((SAMPLE_NUMBER, SAMPLE_NUMBER), jnp.float32),
        ],
        compiler_params=pltpu.CompilerParams(vmem_limit_bytes=12 << 20),
        name="weights",
    )(*pieces)


def analysis_kernel(perturb_ref, mean_ref, *refs):
    routed, out_ref = refs[:4], refs[4]
    mem = lax.axis_index("mem")
    for e in range(4):
        for i in range(2):
            p = (mem - e + 4) % 4 * 2 + i
            update = jnp.dot(routed[e][i], perturb_ref[p], preferred_element_type=jnp.float32)
            out_ref[p] = (mean_ref[p] + update).astype(jnp.bfloat16)


def analysed(perturb, state_mean, routed):
    return pl.pallas_call(
        analysis_kernel,
        out_shape=jax.ShapeDtypeStruct(
            (PATCH_REG, MEMBERS, perturb.shape[2]), jnp.bfloat16
        ),
        compiler_params=pltpu.CompilerParams(vmem_limit_bytes=12 << 20),
        name="analysed",
    )(perturb, state_mean, *routed)


def shift(x, axis, by):
    n = lax.axis_size(axis)
    return lax.ppermute(x, axis, [(j, (j + by) % n) for j in range(n)])


def swap(x, bit):
    return lax.ppermute(x, "mem", [(j, j ^ bit) for j in range(4)])


def per_device(prior, anomalies, spread, departure, tally, zone, tile):
    ways = {a: lax.axis_size(a) for a in ("ylo", "x", "zq", "zp")}
    in_hbm = lambda x: pltpu.with_memory_space_constraint(x, pltpu.HBM)
    messages = build_messages(
        *(in_hbm(x) for x in (anomalies, spread, departure, tally, tile, zone[:, 0])),
        (ways["zq"], ways["ylo"] * ways["x"], ways["zp"]),
    )
    near, far = swap(prior, 1), swap(prior, 2)
    messages, near, far = lax.optimization_barrier((messages, near, far))
    arrived = lax.all_to_all(messages, GROUP, split_axis=0, concat_axis=0, tiled=True)
    arrived, near, far = lax.optimization_barrier((arrived, near, far))
    farther = swap(far, 1)

    pieces = partial_grams(arrived)
    pieces = [pieces[0]] + [shift(pieces[d], "zq", d) for d in range(1, 4)]

    field = jnp.concatenate([prior, near, far, farther], axis=0).transpose(1, 0, 2)
    state_mean = jnp.sum(field, axis=1, keepdims=True, dtype=jnp.float32) / SAMPLE_NUMBER
    perturb = (field - state_mean).astype(jnp.bfloat16)
    pieces, state_mean, perturb = lax.optimization_barrier((pieces, state_mean, perturb))
    weights = flipped_weights(pieces)

    routed = [
        lax.ppermute(
            weights[e],
            ("mem", "zq"),
            [(m * 4 + z, (z + e) % 4 * 4 + m) for m in range(4) for z in range(4)],
        )
        for e in range(4)
    ]
    return analysed(perturb, state_mean, routed).transpose(1, 0, 2)


def solution(mesh):
    grid = Mesh(mesh.devices.reshape(4, 2, 4, 4, 2), ("mem", "ylo", "x", "zq", "zp"))
    return on_grid(grid)


def on_grid(grid):
    reg = ("ylo", "x", "zq", "zp")
    every = ("mem",) + reg
    placed = (
        P("mem", reg, None),
        P(every, None, None),
        P(every, None),
        P(every, None),
        P(every),
        P(every, None),
        P(every),
    )
    return jax.shard_map(
        per_device, mesh=grid, in_specs=placed, out_specs=P("mem", reg, None), check_vma=False
    )
```

```python
import functools
import math

import jax
import jax.numpy as jnp
from jax import lax
from jax.experimental import pallas as pl
from jax.experimental.pallas import tpu as pltpu
from jax.sharding import Mesh
from jax.sharding import PartitionSpec as P


SAMPLE_NUMBER = 256
OB = 128
CAP = 2
PATCH_REG = 8
ITERS = 5
META = 8
ROWS = CAP * OB + META
HALF = SAMPLE_NUMBER // 2
MEMBERS = SAMPLE_NUMBER // 4
PACK = 2 * HALF + 16
GROUP = ("mem", "ylo", "x", "zp")
STEP = 8
TAGS = 16


def prep_kernel(
    ways, zone_smem, tally_smem, tile_smem, anom_ref, spread_ref, depart_ref, out_ref, anom_buf,
    meta_wide, counts, sems
):
    blocks = anom_ref.shape[0]
    regions = out_ref.shape[0]
    zq_ways, plane_ways, zp_ways = ways

    def load(g):
        part = pl.ds(g * STEP, STEP)
        return pltpu.make_async_copy(anom_ref.at[part], anom_buf.at[part], sems.at[g])

    for g in range(blocks // STEP):
        load(g).start()

    @pl.loop(0, regions)
    def _(r):
        counts[r] = 0

    meta_wide[...] = jnp.zeros_like(meta_wide)
    row = lax.broadcasted_iota(jnp.int32, (OB, 1), 0)
    lane = lax.broadcasted_iota(jnp.int32, (1, OB), 1)

    @pl.loop(0, blocks // STEP)
    def _(g):
        part = pl.ds(pl.multiple_of(g * STEP, STEP), STEP)
        spread, depart = spread_ref[part, :], depart_ref[part, :]
        spread_t = spread.T
        load(g).wait()
        for j in range(STEP):
            b = g * STEP + j
            region = zone_smem[b]
            rank = counts[region]
            counts[region] = rank + 1
            rest = region // zp_ways
            place = (rest % zq_ways * plane_ways + rest // zq_ways) * zp_ways + region % zp_ways

            weight = jnp.where(row < tally_smem[b], spread_t[:, j : j + 1], 0.0)
            scaled = anom_buf[b].astype(jnp.float32) * weight
            start = pl.multiple_of(rank * OB, OB)
            out_ref[place, pl.ds(start, OB), :] = scaled.astype(jnp.bfloat16)

            kept = jnp.where(lane < tally_smem[b], spread[j : j + 1], 0.0)
            tag = jnp.full((1, OB), tile_smem[b] + 1, jnp.int32).astype(jnp.float32)
            content = jnp.concatenate([depart[j : j + 1] * kept, tag], axis=1)
            meta_wide[place, pl.ds(rank, 1), :] = content

    out_ref[:, CAP * OB :, :] = meta_wide[...].astype(jnp.bfloat16)


def build_messages(anomalies, spread, departure, tally, tile, zone, ways):
    blocks = anomalies.shape[0]
    regions = math.prod(ways)
    scalars = pl.BlockSpec(memory_space=pltpu.SMEM)
    vectors = pl.BlockSpec(memory_space=pltpu.VMEM)
    return pl.pallas_call(
        functools.partial(prep_kernel, ways),
        out_shape=jax.ShapeDtypeStruct((regions, ROWS, SAMPLE_NUMBER), jnp.bfloat16),
        in_specs=[scalars] * 3 + [pl.BlockSpec(memory_space=pl.ANY)] + [vectors] * 2,
        out_specs=vectors,
        scratch_shapes=[
            pltpu.VMEM((blocks, OB, SAMPLE_NUMBER), jnp.bfloat16),
            pltpu.VMEM((regions, META, SAMPLE_NUMBER), jnp.float32),
            pltpu.SMEM((regions,), jnp.int32),
            pltpu.SemaphoreType.DMA((blocks // STEP,)),
        ],
        compiler_params=pltpu.CompilerParams(vmem_limit_bytes=24 << 20),
        cost_estimate=pl.CostEstimate(flops=0, bytes_accessed=1 << 23, transcendentals=0),
        name="build_messages",
    )(zone, tally, tile, anomalies, spread, departure)


def high_low(row):
    high = row.astype(jnp.bfloat16)
    return high, (row - high.astype(jnp.float32)).astype(jnp.bfloat16)


def gram_kernel(tag_ref, rows_ref, *refs):
    outs, (upper, corner, tag_vmem, tag_smem, tag_sem) = refs[:4], refs[4:]
    step, zq = pl.program_id(0), lax.axis_index("zq")
    sources = rows_ref.shape[0]

    @pl.when(step == 0)
    def _():
        weight = lax.broadcasted_iota(jnp.int32, tag_ref.shape, 1)
        weight = jnp.where(weight == 0, 1.0, jnp.where(weight == 1, TAGS, 0.0))
        codes = jnp.sum(tag_ref[...].astype(jnp.float32) * weight, axis=1)
        tag_vmem[...] = codes.astype(jnp.int32)
        tag_copy = pltpu.make_async_copy(tag_vmem, tag_smem, tag_sem)
        tag_copy.start()
        upper[...] = jnp.zeros_like(upper)
        corner[...] = jnp.zeros_like(corner)
        tag_copy.wait()

    place = lax.broadcasted_iota(jnp.int32, (META, OB), 0)
    for s in range(sources):
        meta = rows_ref[s, CAP * OB : ROWS, :OB].astype(jnp.float32)
        for i in range(CAP):
            code = tag_smem[step * sources + s, 0]
            tag = (code // TAGS if i else code % TAGS) - 1
            turned = (tag // 2 - zq + 4) % 4 * 2 + tag % 2
            tag = jnp.where(tag >= 0, turned, PATCH_REG)
            block = rows_ref[s, i * OB : (i + 1) * OB, :]
            flipped = block.T
            innovation = jnp.where(place == i, meta, 0.0).astype(jnp.bfloat16)
            left = jnp.concatenate([flipped[:HALF], innovation], axis=0)
            upper[tag] += jnp.dot(left, block, preferred_element_type=jnp.float32)
            corner[tag] += jnp.dot(
                flipped[HALF:], block[:, HALF:], preferred_element_type=jnp.float32
            )

    @pl.when(step == pl.num_programs(0) - 1)
    def _():
        row = lax.broadcasted_iota(jnp.int32, (HALF, HALF), 0)
        col = lax.broadcasted_iota(jnp.int32, (HALF, HALF), 1)
        for p in range(PATCH_REG):
            first, last = upper[p, :HALF, :HALF], corner[p]
            mixed = jnp.where(row >= col, first, last)
            diagonal = jnp.sum(jnp.where(row == col, last, 0.0), axis=0, keepdims=True)
            drive = jnp.sum(upper[p, HALF:, :], axis=0, keepdims=True)
            extra = jnp.concatenate([diagonal, drive[:, :HALF], drive[:, HALF:]], axis=0)
            high, low = high_low(extra)
            tail = jnp.concatenate(
                [
                    high.astype(jnp.float32),
                    low.astype(jnp.float32),
                    jnp.zeros((PACK - 2 * HALF - 6, HALF), jnp.float32),
                ],
                axis=0,
            )
            out = outs[p // 2]
            out[p % 2, :HALF, :] = upper[p, :HALF, HALF:].astype(jnp.bfloat16)
            out[p % 2, HALF : 2 * HALF, :] = mixed.astype(jnp.bfloat16)
            out[p % 2, 2 * HALF :, :] = tail.astype(jnp.bfloat16)


def partial_grams(messages):
    regions = messages.shape[0]
    sources = min(8, regions)
    piece = jax.ShapeDtypeStruct((2, PACK, HALF), jnp.bfloat16)
    return pl.pallas_call(
        gram_kernel,
        out_shape=[piece] * 4,
        grid_spec=pl.GridSpec(
            grid=(regions // sources,),
            in_specs=[
                pl.BlockSpec((regions, META, OB), lambda i: (0, CAP * OB // META, 1)),
                pl.BlockSpec((sources, ROWS, SAMPLE_NUMBER), lambda i: (i, 0, 0)),
            ],
            out_specs=[pl.BlockSpec((2, PACK, HALF), lambda i: (0, 0, 0))] * 4,
            scratch_shapes=[
                pltpu.VMEM((PATCH_REG + 1, HALF + META, SAMPLE_NUMBER), jnp.float32),
                pltpu.VMEM((PATCH_REG + 1, HALF, HALF), jnp.float32),
                pltpu.VMEM((regions, OB), jnp.int32),
                pltpu.SMEM((regions, OB), jnp.int32),
                pltpu.SemaphoreType.DMA,
            ],
        ),
        compiler_params=pltpu.CompilerParams(vmem_limit_bytes=12 << 20),
        cost_estimate=pl.CostEstimate(flops=1 << 31, bytes_accessed=1 << 23, transcendentals=0),
        name="partial_grams",
    )(messages, messages)


def split(a):
    high = a.astype(jnp.bfloat16)
    return high, (a - high.astype(jnp.float32)).astype(jnp.bfloat16)


def product(a, b):
    dot = functools.partial(jnp.dot, preferred_element_type=jnp.float32)
    return dot(a[0], b[0]) + (dot(a[0], b[1]) + dot(a[1], b[0]))


def newton_kernel(a_ref, b_ref, c_ref, d_ref, *refs):
    mem = lax.axis_index("mem")
    outs, (gram_ref, weight_ref) = refs[:4], refs[4:]
    row = lax.broadcasted_iota(jnp.int32, (HALF, HALF), 0)
    col = lax.broadcasted_iota(jnp.int32, (HALF, HALF), 1)
    row_full = lax.broadcasted_iota(jnp.int32, (SAMPLE_NUMBER, SAMPLE_NUMBER), 0)
    col_full = lax.broadcasted_iota(jnp.int32, (SAMPLE_NUMBER, SAMPLE_NUMBER), 1)
    identity = jnp.where(row_full == col_full, 1.0, 0.0)
    for p in range(2):
        total = sum(ref[p].astype(jnp.float32) for ref in (a_ref, b_ref, c_ref, d_ref))
        cross, mixed, tail = total[:HALF], total[HALF : 2 * HALF], total[2 * HALF :]
        extra = tail[0:3] + tail[3:6]
        turned = mixed.T
        gram_ref[p, :HALF, :HALF] = jnp.where(row >= col, mixed, turned)
        gram_ref[p, :HALF, HALF:] = cross
        gram_ref[p, HALF:, :HALF] = cross.T
        gram_ref[p, HALF:, HALF:] = jnp.where(
            row == col, extra[0:1], jnp.where(row < col, mixed, turned)
        )
        drive = jnp.concatenate([extra[1:2], extra[2:3]], axis=1)
        gram = gram_ref[p] + (SAMPLE_NUMBER - 1.0) * identity
        squares = jnp.sum(jnp.sum(gram * gram, axis=0, keepdims=True), axis=1, keepdims=True)
        frob = jnp.sqrt(squares)
        root = gram / frob
        inverse = step = 1.5 * identity - 0.5 * root
        for _ in range(1, ITERS):
            step_parts = split(step)
            root = product(split(root), step_parts)
            inverse_parts = split(inverse)
            step = 1.5 * identity - 0.5 * product(inverse_parts, split(root))
            inverse = product(split(step), inverse_parts)
        inv_root = inverse / jnp.sqrt(frob)
        once = jnp.sum(inv_root * drive, axis=1, keepdims=True)
        mean_weight = jnp.sum(inv_root * once, axis=0, keepdims=True)
        weight_ref[...] = math.sqrt(SAMPLE_NUMBER - 1.0) * inv_root + mean_weight
        for e in range(4):
            goal = mem ^ e
            part = weight_ref[pl.ds(pl.multiple_of(goal * MEMBERS, MEMBERS), MEMBERS), :]
            low, high = part[:, :HALF], part[:, HALF:]
            low, high = jnp.where(goal >= 2, high, low), jnp.where(goal >= 2, low, high)
            for i, side in enumerate((low, high)):
                side = jnp.where(goal % 2 == 1, pltpu.roll(side, MEMBERS, 1), side)
                outs[e][p, :, i * HALF : (i + 1) * HALF] = side.astype(jnp.bfloat16)


def flipped_weights(pieces):
    piece = jax.ShapeDtypeStruct((2, MEMBERS, SAMPLE_NUMBER), jnp.bfloat16)
    return pl.pallas_call(
        newton_kernel,
        out_shape=[piece] * 4,
        scratch_shapes=[
            pltpu.VMEM((2, SAMPLE_NUMBER, SAMPLE_NUMBER), jnp.float32),
            pltpu.VMEM((SAMPLE_NUMBER, SAMPLE_NUMBER), jnp.float32),
        ],
        compiler_params=pltpu.CompilerParams(vmem_limit_bytes=12 << 20),
        name="weights",
    )(*pieces)


def analysis_kernel(perturb_ref, mean_ref, *refs):
    routed, out_ref = refs[:4], refs[4]
    mem = lax.axis_index("mem")
    for e in range(4):
        for i in range(2):
            p = (mem ^ e) * 2 + i
            update = jnp.dot(routed[e][i], perturb_ref[p], preferred_element_type=jnp.float32)
            out_ref[p] = (mean_ref[p] + update).astype(jnp.bfloat16)


def analysed(perturb, state_mean, routed):
    return pl.pallas_call(
        analysis_kernel,
        out_shape=jax.ShapeDtypeStruct(
            (PATCH_REG, MEMBERS, perturb.shape[2]), jnp.bfloat16
        ),
        compiler_params=pltpu.CompilerParams(vmem_limit_bytes=12 << 20),
        name="analysed",
    )(perturb, state_mean, *routed)


def swap(x, bit):
    return lax.ppermute(x, "mem", [(j, j ^ bit) for j in range(4)])


def to_owner(x, e):
    pairs = [(m * 4 + z, (z + e) % 4 * 4 + m) for m in range(4) for z in range(4)]
    return lax.ppermute(x, ("mem", "zq"), pairs)


def per_device(prior, anomalies, spread, departure, tally, zone, tile):
    ways = {a: lax.axis_size(a) for a in ("ylo", "x", "zq", "zp")}
    in_hbm = lambda x: pltpu.with_memory_space_constraint(x, pltpu.HBM)
    messages = build_messages(
        *(in_hbm(x) for x in (anomalies, spread, departure, tally, tile, zone[:, 0])),
        (ways["zq"], ways["ylo"] * ways["x"], ways["zp"]),
    )
    arrived = lax.all_to_all(messages, GROUP, split_axis=0, concat_axis=0, tiled=True)

    pieces = partial_grams(arrived)
    pieces, prior = lax.optimization_barrier((pieces, prior))
    pieces = [to_owner(pieces[e], e) for e in range(4)]

    near, far = swap(prior, 1), swap(prior, 2)
    farther = swap(far, 1)
    field = jnp.concatenate([prior, near, far, farther], axis=0).transpose(1, 0, 2)
    state_mean = jnp.sum(field, axis=1, keepdims=True, dtype=jnp.float32) / SAMPLE_NUMBER
    perturb = (field - state_mean).astype(jnp.bfloat16)

    weights = flipped_weights(pieces)
    routed = [weights[0]] + [swap(weights[e], e) for e in range(1, 4)]
    return analysed(perturb, state_mean, routed).transpose(1, 0, 2)


def solution(mesh):
    grid = Mesh(mesh.devices.reshape(4, 2, 4, 4, 2), ("mem", "ylo", "x", "zq", "zp"))
    return on_grid(grid)


def on_grid(grid):
    reg = ("ylo", "x", "zq", "zp")
    every = ("mem",) + reg
    placed = (
        P("mem", reg, None),
        P(every, None, None),
        P(every, None),
        P(every, None),
        P(every),
        P(every, None),
        P(every),
    )
    return jax.shard_map(
        per_device, mesh=grid, in_specs=placed, out_specs=P("mem", reg, None), check_vma=False
    )
```

```python
import functools
import math

import jax
import jax.numpy as jnp
from jax import lax
from jax.experimental import pallas as pl
from jax.experimental.pallas import tpu as pltpu
from jax.sharding import Mesh
from jax.sharding import PartitionSpec as P


SAMPLE_NUMBER = 256
OB = 128
CAP = 2
PATCH_REG = 8
ITERS = 5
META = 8
ROWS = CAP * OB + META
HALF = SAMPLE_NUMBER // 2
MEMBERS = SAMPLE_NUMBER // 4
PACK = 2 * HALF + 16
GROUP = ("mem", "ylo", "x", "zp")
STEP = 8
TAGS = 16


def prep_kernel(
    ways, zone_smem, tally_smem, tile_smem, anom_ref, spread_ref, depart_ref, out_ref, anom_buf,
    meta_wide, counts, sems
):
    blocks = anom_ref.shape[0]
    regions = out_ref.shape[0]
    zq_ways, plane_ways, zp_ways = ways

    def load(g):
        part = pl.ds(g * STEP, STEP)
        return pltpu.make_async_copy(anom_ref.at[part], anom_buf.at[part], sems.at[g])

    for g in range(blocks // STEP):
        load(g).start()

    @pl.loop(0, regions)
    def _(r):
        counts[r] = 0

    meta_wide[...] = jnp.zeros_like(meta_wide)
    row = lax.broadcasted_iota(jnp.int32, (OB, 1), 0)
    lane = lax.broadcasted_iota(jnp.int32, (1, OB), 1)

    @pl.loop(0, blocks // STEP)
    def _(g):
        part = pl.ds(pl.multiple_of(g * STEP, STEP), STEP)
        spread, depart = spread_ref[part, :], depart_ref[part, :]
        spread_t = spread.T
        load(g).wait()
        for j in range(STEP):
            b = g * STEP + j
            region = zone_smem[b]
            rank = counts[region]
            counts[region] = rank + 1
            rest = region // zp_ways
            place = (rest % zq_ways * plane_ways + rest // zq_ways) * zp_ways + region % zp_ways

            weight = jnp.where(row < tally_smem[b], spread_t[:, j : j + 1], 0.0)
            scaled = anom_buf[b].astype(jnp.float32) * weight
            start = pl.multiple_of(rank * OB, OB)
            out_ref[place, pl.ds(start, OB), :] = scaled.astype(jnp.bfloat16)

            kept = jnp.where(lane < tally_smem[b], spread[j : j + 1], 0.0)
            tag = jnp.full((1, OB), tile_smem[b] + 1, jnp.int32).astype(jnp.float32)
            content = jnp.concatenate([depart[j : j + 1] * kept, tag], axis=1)
            meta_wide[place, pl.ds(rank, 1), :] = content

    out_ref[:, CAP * OB :, :] = meta_wide[...].astype(jnp.bfloat16)


def build_messages(anomalies, spread, departure, tally, tile, zone, ways):
    blocks = anomalies.shape[0]
    regions = math.prod(ways)
    scalars = pl.BlockSpec(memory_space=pltpu.SMEM)
    vectors = pl.BlockSpec(memory_space=pltpu.VMEM)
    return pl.pallas_call(
        functools.partial(prep_kernel, ways),
        out_shape=jax.ShapeDtypeStruct((regions, ROWS, SAMPLE_NUMBER), jnp.bfloat16),
        in_specs=[scalars] * 3 + [pl.BlockSpec(memory_space=pl.ANY)] + [vectors] * 2,
        out_specs=vectors,
        scratch_shapes=[
            pltpu.VMEM((blocks, OB, SAMPLE_NUMBER), jnp.bfloat16),
            pltpu.VMEM((regions, META, SAMPLE_NUMBER), jnp.float32),
            pltpu.SMEM((regions,), jnp.int32),
            pltpu.SemaphoreType.DMA((blocks // STEP,)),
        ],
        compiler_params=pltpu.CompilerParams(vmem_limit_bytes=24 << 20),
        cost_estimate=pl.CostEstimate(flops=0, bytes_accessed=1 << 23, transcendentals=0),
        name="build_messages",
    )(zone, tally, tile, anomalies, spread, departure)


def high_low(row):
    high = row.astype(jnp.bfloat16)
    return high, (row - high.astype(jnp.float32)).astype(jnp.bfloat16)


def gram_kernel(tag_ref, rows_ref, *refs):
    outs, (upper, corner, tag_vmem, tag_smem, tag_sem) = refs[:4], refs[4:]
    step, zq = pl.program_id(0), lax.axis_index("zq")
    sources = rows_ref.shape[0]

    @pl.when(step == 0)
    def _():
        weight = lax.broadcasted_iota(jnp.int32, tag_ref.shape, 1)
        weight = jnp.where(weight == 0, 1.0, jnp.where(weight == 1, TAGS, 0.0))
        codes = jnp.sum(tag_ref[...].astype(jnp.float32) * weight, axis=1)
        tag_vmem[...] = codes.astype(jnp.int32)
        tag_copy = pltpu.make_async_copy(tag_vmem, tag_smem, tag_sem)
        tag_copy.start()
        upper[...] = jnp.zeros_like(upper)
        corner[...] = jnp.zeros_like(corner)
        tag_copy.wait()

    place = lax.broadcasted_iota(jnp.int32, (META, OB), 0)
    for s in range(sources):
        meta = rows_ref[s, CAP * OB : ROWS, :OB].astype(jnp.float32)
        for i in range(CAP):
            code = tag_smem[step * sources + s, 0]
            tag = (code // TAGS if i else code % TAGS) - 1
            turned = (tag // 2 - zq + 4) % 4 * 2 + tag % 2
            tag = jnp.where(tag >= 0, turned, PATCH_REG)
            block = rows_ref[s, i * OB : (i + 1) * OB, :]
            flipped = block.T
            innovation = jnp.where(place == i, meta, 0.0).astype(jnp.bfloat16)
            left = jnp.concatenate([flipped[:HALF], innovation], axis=0)
            upper[tag] += jnp.dot(left, block, preferred_element_type=jnp.float32)
            corner[tag] += jnp.dot(
                flipped[HALF:], block[:, HALF:], preferred_element_type=jnp.float32
            )

    @pl.when(step == pl.num_programs(0) - 1)
    def _():
        row = lax.broadcasted_iota(jnp.int32, (HALF, HALF), 0)
        col = lax.broadcasted_iota(jnp.int32, (HALF, HALF), 1)
        for p in range(PATCH_REG):
            first, last = upper[p, :HALF, :HALF], corner[p]
            mixed = jnp.where(row >= col, first, last)
            diagonal = jnp.sum(jnp.where(row == col, last, 0.0), axis=0, keepdims=True)
            drive = jnp.sum(upper[p, HALF:, :], axis=0, keepdims=True)
            extra = jnp.concatenate([diagonal, drive[:, :HALF], drive[:, HALF:]], axis=0)
            high, low = high_low(extra)
            tail = jnp.concatenate(
                [
                    high.astype(jnp.float32),
                    low.astype(jnp.float32),
                    jnp.zeros((PACK - 2 * HALF - 6, HALF), jnp.float32),
                ],
                axis=0,
            )
            out = outs[p // 2]
            out[p % 2, :HALF, :] = upper[p, :HALF, HALF:].astype(jnp.bfloat16)
            out[p % 2, HALF : 2 * HALF, :] = mixed.astype(jnp.bfloat16)
            out[p % 2, 2 * HALF :, :] = tail.astype(jnp.bfloat16)


def partial_grams(messages):
    regions = messages.shape[0]
    sources = min(8, regions)
    piece = jax.ShapeDtypeStruct((2, PACK, HALF), jnp.bfloat16)
    return pl.pallas_call(
        gram_kernel,
        out_shape=[piece] * 4,
        grid_spec=pl.GridSpec(
            grid=(regions // sources,),
            in_specs=[
                pl.BlockSpec((regions, META, OB), lambda i: (0, CAP * OB // META, 1)),
                pl.BlockSpec((sources, ROWS, SAMPLE_NUMBER), lambda i: (i, 0, 0)),
            ],
            out_specs=[pl.BlockSpec((2, PACK, HALF), lambda i: (0, 0, 0))] * 4,
            scratch_shapes=[
                pltpu.VMEM((PATCH_REG + 1, HALF + META, SAMPLE_NUMBER), jnp.float32),
                pltpu.VMEM((PATCH_REG + 1, HALF, HALF), jnp.float32),
                pltpu.VMEM((regions, OB), jnp.int32),
                pltpu.SMEM((regions, OB), jnp.int32),
                pltpu.SemaphoreType.DMA,
            ],
        ),
        compiler_params=pltpu.CompilerParams(vmem_limit_bytes=12 << 20),
        cost_estimate=pl.CostEstimate(flops=1 << 31, bytes_accessed=1 << 23, transcendentals=0),
        name="partial_grams",
    )(messages, messages)


def split(a):
    high = a.astype(jnp.bfloat16)
    return high, (a - high.astype(jnp.float32)).astype(jnp.bfloat16)


def product(a, b):
    dot = functools.partial(jnp.dot, preferred_element_type=jnp.float32)
    return dot(a[0], b[0]) + (dot(a[0], b[1]) + dot(a[1], b[0]))


def newton_kernel(a_ref, b_ref, c_ref, d_ref, *refs):
    mem = lax.axis_index("mem")
    outs, (gram_ref, weight_ref) = refs[:4], refs[4:]
    row = lax.broadcasted_iota(jnp.int32, (HALF, HALF), 0)
    col = lax.broadcasted_iota(jnp.int32, (HALF, HALF), 1)
    row_full = lax.broadcasted_iota(jnp.int32, (SAMPLE_NUMBER, SAMPLE_NUMBER), 0)
    col_full = lax.broadcasted_iota(jnp.int32, (SAMPLE_NUMBER, SAMPLE_NUMBER), 1)
    identity = jnp.where(row_full == col_full, 1.0, 0.0)
    for p in range(2):
        total = sum(ref[p].astype(jnp.float32) for ref in (a_ref, b_ref, c_ref, d_ref))
        cross, mixed, tail = total[:HALF], total[HALF : 2 * HALF], total[2 * HALF :]
        extra = tail[0:3] + tail[3:6]
        turned = mixed.T
        gram_ref[p, :HALF, :HALF] = jnp.where(row >= col, mixed, turned)
        gram_ref[p, :HALF, HALF:] = cross
        gram_ref[p, HALF:, :HALF] = cross.T
        gram_ref[p, HALF:, HALF:] = jnp.where(
            row == col, extra[0:1], jnp.where(row < col, mixed, turned)
        )
        drive = jnp.concatenate([extra[1:2], extra[2:3]], axis=1)
        gram = gram_ref[p] + (SAMPLE_NUMBER - 1.0) * identity
        squares = jnp.sum(jnp.sum(gram * gram, axis=0, keepdims=True), axis=1, keepdims=True)
        frob = jnp.sqrt(squares)
        root = gram / frob
        inverse = step = 1.5 * identity - 0.5 * root
        for _ in range(1, ITERS):
            step_parts = split(step)
            root = product(split(root), step_parts)
            inverse_parts = split(inverse)
            step = 1.5 * identity - 0.5 * product(inverse_parts, split(root))
            inverse = product(split(step), inverse_parts)
        inv_root = inverse / jnp.sqrt(frob)
        once = jnp.sum(inv_root * drive, axis=1, keepdims=True)
        mean_weight = jnp.sum(inv_root * once, axis=0, keepdims=True)
        weight_ref[...] = math.sqrt(SAMPLE_NUMBER - 1.0) * inv_root + mean_weight
        for e in range(4):
            goal = mem ^ e
            part = weight_ref[pl.ds(pl.multiple_of(goal * MEMBERS, MEMBERS), MEMBERS), :]
            low, high = part[:, :HALF], part[:, HALF:]
            low, high = jnp.where(goal >= 2, high, low), jnp.where(goal >= 2, low, high)
            for i, side in enumerate((low, high)):
                side = jnp.where(goal % 2 == 1, pltpu.roll(side, MEMBERS, 1), side)
                outs[e][p, :, i * HALF : (i + 1) * HALF] = side.astype(jnp.bfloat16)


def flipped_weights(pieces):
    piece = jax.ShapeDtypeStruct((2, MEMBERS, SAMPLE_NUMBER), jnp.bfloat16)
    return pl.pallas_call(
        newton_kernel,
        out_shape=[piece] * 4,
        scratch_shapes=[
            pltpu.VMEM((2, SAMPLE_NUMBER, SAMPLE_NUMBER), jnp.float32),
            pltpu.VMEM((SAMPLE_NUMBER, SAMPLE_NUMBER), jnp.float32),
        ],
        compiler_params=pltpu.CompilerParams(vmem_limit_bytes=12 << 20),
        name="weights",
    )(*pieces)


def analysis_kernel(perturb_ref, mean_ref, *refs):
    routed, out_ref = refs[:4], refs[4]
    mem = lax.axis_index("mem")
    for e in range(4):
        for i in range(2):
            p = (mem ^ e) * 2 + i
            update = jnp.dot(routed[e][i], perturb_ref[p], preferred_element_type=jnp.float32)
            out_ref[p] = (mean_ref[p] + update).astype(jnp.bfloat16)


def analysed(perturb, state_mean, routed):
    return pl.pallas_call(
        analysis_kernel,
        out_shape=jax.ShapeDtypeStruct(
            (PATCH_REG, MEMBERS, perturb.shape[2]), jnp.bfloat16
        ),
        compiler_params=pltpu.CompilerParams(vmem_limit_bytes=12 << 20),
        name="analysed",
    )(perturb, state_mean, *routed)


def swap(x, bit):
    return lax.ppermute(x, "mem", [(j, j ^ bit) for j in range(4)])


def to_owner(x, e):
    pairs = [(m * 4 + z, (z + e) % 4 * 4 + m) for m in range(4) for z in range(4)]
    return lax.ppermute(x, ("mem", "zq"), pairs)


def per_device(prior, anomalies, spread, departure, tally, zone, tile):
    ways = {a: lax.axis_size(a) for a in ("ylo", "x", "zq", "zp")}
    in_hbm = lambda x: pltpu.with_memory_space_constraint(x, pltpu.HBM)
    messages = build_messages(
        *(in_hbm(x) for x in (anomalies, spread, departure, tally, tile, zone[:, 0])),
        (ways["zq"], ways["ylo"] * ways["x"], ways["zp"]),
    )
    arrived = lax.all_to_all(messages, GROUP, split_axis=0, concat_axis=0, tiled=True)

    arrived, prior = lax.optimization_barrier((arrived, prior))
    near, far = swap(prior, 1), swap(prior, 2)

    pieces = partial_grams(arrived)
    weights = flipped_weights([to_owner(pieces[e], e) for e in range(4)])

    weights, far = lax.optimization_barrier((weights, far))
    routed = [weights[0]] + [swap(weights[e], e) for e in range(1, 4)]
    farther = swap(far, 1)
    field = jnp.concatenate([prior, near, far, farther], axis=0).transpose(1, 0, 2)
    state_mean = jnp.sum(field, axis=1, keepdims=True, dtype=jnp.float32) / SAMPLE_NUMBER
    perturb = (field - state_mean).astype(jnp.bfloat16)
    return analysed(perturb, state_mean, routed).transpose(1, 0, 2)


def solution(mesh):
    grid = Mesh(mesh.devices.reshape(4, 2, 4, 4, 2), ("mem", "ylo", "x", "zq", "zp"))
    return on_grid(grid)


def on_grid(grid):
    reg = ("ylo", "x", "zq", "zp")
    every = ("mem",) + reg
    placed = (
        P("mem", reg, None),
        P(every, None, None),
        P(every, None),
        P(every, None),
        P(every),
        P(every, None),
        P(every),
    )
    return jax.shard_map(
        per_device, mesh=grid, in_specs=placed, out_specs=P("mem", reg, None), check_vma=False
    )
```

```python
import functools
import math

import jax
import jax.numpy as jnp
from jax import lax
from jax.experimental import pallas as pl
from jax.experimental.pallas import tpu as pltpu
from jax.sharding import Mesh
from jax.sharding import PartitionSpec as P


SAMPLE_NUMBER = 256
OB = 128
CAP = 2
PATCH_REG = 8
ITERS = 5
META = 8
ROWS = CAP * OB + META
HALF = SAMPLE_NUMBER // 2
MEMBERS = SAMPLE_NUMBER // 4
PACK = 2 * HALF + 16
GROUP = ("mem", "ylo", "x", "zp")
STEP = 8
ALONG = (0, 2, 1, 3)
TAGS = 16


def prep_kernel(
    ways, zone_smem, tally_smem, tile_smem, anom_ref, spread_ref, depart_ref, out_ref, anom_buf,
    meta_wide, counts, sems
):
    blocks = anom_ref.shape[0]
    regions = out_ref.shape[0]
    zq_ways, plane_ways, zp_ways = ways
    zq = lax.axis_index("zq")

    def load(g):
        part = pl.ds(g * STEP, STEP)
        return pltpu.make_async_copy(anom_ref.at[part], anom_buf.at[part], sems.at[g])

    for g in range(blocks // STEP):
        load(g).start()

    @pl.loop(0, regions)
    def _(r):
        counts[r] = 0

    meta_wide[...] = jnp.zeros_like(meta_wide)
    row = lax.broadcasted_iota(jnp.int32, (OB, 1), 0)
    lane = lax.broadcasted_iota(jnp.int32, (1, OB), 1)

    @pl.loop(0, blocks // STEP)
    def _(g):
        part = pl.ds(pl.multiple_of(g * STEP, STEP), STEP)
        spread, depart = spread_ref[part, :], depart_ref[part, :]
        spread_t = spread.T
        load(g).wait()
        for j in range(STEP):
            b = g * STEP + j
            region = zone_smem[b]
            rank = counts[region]
            counts[region] = rank + 1
            rest = region // zp_ways
            along = (rest % zq_ways - zq + zq_ways) % zq_ways
            mem = along % 2 * 2 + along // 2
            place = (mem * plane_ways + rest // zq_ways) * zp_ways + region % zp_ways

            weight = jnp.where(row < tally_smem[b], spread_t[:, j : j + 1], 0.0)
            scaled = anom_buf[b].astype(jnp.float32) * weight
            start = pl.multiple_of(rank * OB, OB)
            out_ref[place, pl.ds(start, OB), :] = scaled.astype(jnp.bfloat16)

            kept = jnp.where(lane < tally_smem[b], spread[j : j + 1], 0.0)
            tag = jnp.full((1, OB), tile_smem[b] + 1, jnp.int32).astype(jnp.float32)
            content = jnp.concatenate([depart[j : j + 1] * kept, tag], axis=1)
            meta_wide[place, pl.ds(rank, 1), :] = content

    out_ref[:, CAP * OB :, :] = meta_wide[...].astype(jnp.bfloat16)


def build_messages(anomalies, spread, departure, tally, tile, zone, ways):
    blocks = anomalies.shape[0]
    regions = math.prod(ways)
    scalars = pl.BlockSpec(memory_space=pltpu.SMEM)
    vectors = pl.BlockSpec(memory_space=pltpu.VMEM)
    return pl.pallas_call(
        functools.partial(prep_kernel, ways),
        out_shape=jax.ShapeDtypeStruct((regions, ROWS, SAMPLE_NUMBER), jnp.bfloat16),
        in_specs=[scalars] * 3 + [pl.BlockSpec(memory_space=pl.ANY)] + [vectors] * 2,
        out_specs=vectors,
        scratch_shapes=[
            pltpu.VMEM((blocks, OB, SAMPLE_NUMBER), jnp.bfloat16),
            pltpu.VMEM((regions, META, SAMPLE_NUMBER), jnp.float32),
            pltpu.SMEM((regions,), jnp.int32),
            pltpu.SemaphoreType.DMA((blocks // STEP,)),
        ],
        compiler_params=pltpu.CompilerParams(vmem_limit_bytes=24 << 20),
        cost_estimate=pl.CostEstimate(flops=0, bytes_accessed=1 << 23, transcendentals=0),
        name="build_messages",
    )(zone, tally, tile, anomalies, spread, departure)


def high_low(row):
    high = row.astype(jnp.bfloat16)
    return high, (row - high.astype(jnp.float32)).astype(jnp.bfloat16)


def gram_kernel(tag_ref, rows_ref, *refs):
    outs, (upper, corner, tag_vmem, tag_smem, tag_sem) = refs[:4], refs[4:]
    step, mem = pl.program_id(0), lax.axis_index("mem")
    sources = rows_ref.shape[0]

    @pl.when(step == 0)
    def _():
        weight = lax.broadcasted_iota(jnp.int32, tag_ref.shape, 1)
        weight = jnp.where(weight == 0, 1.0, jnp.where(weight == 1, TAGS, 0.0))
        codes = jnp.sum(tag_ref[...].astype(jnp.float32) * weight, axis=1)
        tag_vmem[...] = codes.astype(jnp.int32)
        tag_copy = pltpu.make_async_copy(tag_vmem, tag_smem, tag_sem)
        tag_copy.start()
        upper[...] = jnp.zeros_like(upper)
        corner[...] = jnp.zeros_like(corner)
        tag_copy.wait()

    place = lax.broadcasted_iota(jnp.int32, (META, OB), 0)
    for s in range(sources):
        meta = rows_ref[s, CAP * OB : ROWS, :OB].astype(jnp.float32)
        for i in range(CAP):
            code = tag_smem[step * sources + s, 0]
            tag = (code // TAGS if i else code % TAGS) - 1
            turned = ((tag // 2) ^ mem) * 2 + tag % 2
            tag = jnp.where(tag >= 0, turned, PATCH_REG)
            block = rows_ref[s, i * OB : (i + 1) * OB, :]
            flipped = block.T
            innovation = jnp.where(place == i, meta, 0.0).astype(jnp.bfloat16)
            left = jnp.concatenate([flipped[:HALF], innovation], axis=0)
            upper[tag] += jnp.dot(left, block, preferred_element_type=jnp.float32)
            corner[tag] += jnp.dot(
                flipped[HALF:], block[:, HALF:], preferred_element_type=jnp.float32
            )

    @pl.when(step == pl.num_programs(0) - 1)
    def _():
        row = lax.broadcasted_iota(jnp.int32, (HALF, HALF), 0)
        col = lax.broadcasted_iota(jnp.int32, (HALF, HALF), 1)
        for p in range(PATCH_REG):
            first, last = upper[p, :HALF, :HALF], corner[p]
            mixed = jnp.where(row >= col, first, last)
            diagonal = jnp.sum(jnp.where(row == col, last, 0.0), axis=0, keepdims=True)
            drive = jnp.sum(upper[p, HALF:, :], axis=0, keepdims=True)
            extra = jnp.concatenate([diagonal, drive[:, :HALF], drive[:, HALF:]], axis=0)
            high, low = high_low(extra)
            tail = jnp.concatenate(
                [
                    high.astype(jnp.float32),
                    low.astype(jnp.float32),
                    jnp.zeros((PACK - 2 * HALF - 6, HALF), jnp.float32),
                ],
                axis=0,
            )
            out = outs[p // 2]
            out[p % 2, :HALF, :] = upper[p, :HALF, HALF:].astype(jnp.bfloat16)
            out[p % 2, HALF : 2 * HALF, :] = mixed.astype(jnp.bfloat16)
            out[p % 2, 2 * HALF :, :] = tail.astype(jnp.bfloat16)


def partial_grams(messages):
    regions = messages.shape[0]
    sources = min(8, regions)
    piece = jax.ShapeDtypeStruct((2, PACK, HALF), jnp.bfloat16)
    return pl.pallas_call(
        gram_kernel,
        out_shape=[piece] * 4,
        grid_spec=pl.GridSpec(
            grid=(regions // sources,),
            in_specs=[
                pl.BlockSpec((regions, META, OB), lambda i: (0, CAP * OB // META, 1)),
                pl.BlockSpec((sources, ROWS, SAMPLE_NUMBER), lambda i: (i, 0, 0)),
            ],
            out_specs=[pl.BlockSpec((2, PACK, HALF), lambda i: (0, 0, 0))] * 4,
            scratch_shapes=[
                pltpu.VMEM((PATCH_REG + 1, HALF + META, SAMPLE_NUMBER), jnp.float32),
                pltpu.VMEM((PATCH_REG + 1, HALF, HALF), jnp.float32),
                pltpu.VMEM((regions, OB), jnp.int32),
                pltpu.SMEM((regions, OB), jnp.int32),
                pltpu.SemaphoreType.DMA,
            ],
        ),
        compiler_params=pltpu.CompilerParams(vmem_limit_bytes=12 << 20),
        cost_estimate=pl.CostEstimate(flops=1 << 31, bytes_accessed=1 << 23, transcendentals=0),
        name="partial_grams",
    )(messages, messages)


def split(a):
    high = a.astype(jnp.bfloat16)
    return high, (a - high.astype(jnp.float32)).astype(jnp.bfloat16)


def product(a, b):
    dot = functools.partial(jnp.dot, preferred_element_type=jnp.float32)
    return dot(a[0], b[0]) + (dot(a[0], b[1]) + dot(a[1], b[0]))


def newton_kernel(a_ref, b_ref, c_ref, d_ref, *refs):
    mem = lax.axis_index("mem")
    outs, (gram_ref, weight_ref) = refs[:4], refs[4:]
    row = lax.broadcasted_iota(jnp.int32, (HALF, HALF), 0)
    col = lax.broadcasted_iota(jnp.int32, (HALF, HALF), 1)
    row_full = lax.broadcasted_iota(jnp.int32, (SAMPLE_NUMBER, SAMPLE_NUMBER), 0)
    col_full = lax.broadcasted_iota(jnp.int32, (SAMPLE_NUMBER, SAMPLE_NUMBER), 1)
    identity = jnp.where(row_full == col_full, 1.0, 0.0)
    for p in range(2):
        total = sum(ref[p].astype(jnp.float32) for ref in (a_ref, b_ref, c_ref, d_ref))
        cross, mixed, tail = total[:HALF], total[HALF : 2 * HALF], total[2 * HALF :]
        extra = tail[0:3] + tail[3:6]
        turned = mixed.T
        gram_ref[p, :HALF, :HALF] = jnp.where(row >= col, mixed, turned)
        gram_ref[p, :HALF, HALF:] = cross
        gram_ref[p, HALF:, :HALF] = cross.T
        gram_ref[p, HALF:, HALF:] = jnp.where(
            row == col, extra[0:1], jnp.where(row < col, mixed, turned)
        )
        drive = jnp.concatenate([extra[1:2], extra[2:3]], axis=1)
        gram = gram_ref[p] + (SAMPLE_NUMBER - 1.0) * identity
        squares = jnp.sum(jnp.sum(gram * gram, axis=0, keepdims=True), axis=1, keepdims=True)
        frob = jnp.sqrt(squares)
        root = gram / frob
        inverse = step = 1.5 * identity - 0.5 * root
        for _ in range(1, ITERS):
            step_parts = split(step)
            root = product(split(root), step_parts)
            inverse_parts = split(inverse)
            step = 1.5 * identity - 0.5 * product(inverse_parts, split(root))
            inverse = product(split(step), inverse_parts)
        inv_root = inverse / jnp.sqrt(frob)
        once = jnp.sum(inv_root * drive, axis=1, keepdims=True)
        mean_weight = jnp.sum(inv_root * once, axis=0, keepdims=True)
        weight_ref[...] = math.sqrt(SAMPLE_NUMBER - 1.0) * inv_root + mean_weight
        for e in range(4):
            goal = mem ^ e
            part = weight_ref[pl.ds(pl.multiple_of(goal * MEMBERS, MEMBERS), MEMBERS), :]
            low, high = part[:, :HALF], part[:, HALF:]
            low, high = jnp.where(goal >= 2, high, low), jnp.where(goal >= 2, low, high)
            for i, side in enumerate((low, high)):
                side = jnp.where(goal % 2 == 1, pltpu.roll(side, MEMBERS, 1), side)
                outs[e][p, :, i * HALF : (i + 1) * HALF] = side.astype(jnp.bfloat16)


def flipped_weights(pieces):
    piece = jax.ShapeDtypeStruct((2, MEMBERS, SAMPLE_NUMBER), jnp.bfloat16)
    return pl.pallas_call(
        newton_kernel,
        out_shape=[piece] * 4,
        scratch_shapes=[
            pltpu.VMEM((2, SAMPLE_NUMBER, SAMPLE_NUMBER), jnp.float32),
            pltpu.VMEM((SAMPLE_NUMBER, SAMPLE_NUMBER), jnp.float32),
        ],
        compiler_params=pltpu.CompilerParams(vmem_limit_bytes=12 << 20),
        name="weights",
    )(*pieces)


def analysis_kernel(perturb_ref, mean_ref, *refs):
    routed, out_ref = refs[:4], refs[4]
    mem = lax.axis_index("mem")
    for e in range(4):
        for i in range(2):
            p = (mem ^ e) * 2 + i
            update = jnp.dot(routed[e][i], perturb_ref[p], preferred_element_type=jnp.float32)
            out_ref[p] = (mean_ref[p] + update).astype(jnp.bfloat16)


def analysed(perturb, state_mean, routed):
    return pl.pallas_call(
        analysis_kernel,
        out_shape=jax.ShapeDtypeStruct(
            (PATCH_REG, MEMBERS, perturb.shape[2]), jnp.bfloat16
        ),
        compiler_params=pltpu.CompilerParams(vmem_limit_bytes=12 << 20),
        name="analysed",
    )(perturb, state_mean, *routed)


def swap(x, bit):
    return lax.ppermute(x, "mem", [(j, j ^ bit) for j in range(4)])


def to_owner(x, e):
    pairs = [(m * 4 + z, (m ^ e) * 4 + (z + ALONG[m]) % 4) for m in range(4) for z in range(4)]
    return lax.ppermute(x, ("mem", "zq"), pairs)


def per_device(prior, anomalies, spread, departure, tally, zone, tile):
    ways = {a: lax.axis_size(a) for a in ("ylo", "x", "zq", "zp")}
    in_hbm = lambda x: pltpu.with_memory_space_constraint(x, pltpu.HBM)
    messages = build_messages(
        *(in_hbm(x) for x in (anomalies, spread, departure, tally, tile, zone[:, 0])),
        (ways["zq"], ways["ylo"] * ways["x"], ways["zp"]),
    )
    arrived = lax.all_to_all(messages, GROUP, split_axis=0, concat_axis=0, tiled=True)

    arrived, prior = lax.optimization_barrier((arrived, prior))
    near, far = swap(prior, 1), swap(prior, 2)

    pieces = partial_grams(arrived)
    pieces = [to_owner(pieces[e], e) for e in range(4)]

    farther = swap(far, 1)
    field = jnp.concatenate([prior, near, far, farther], axis=0).transpose(1, 0, 2)
    state_mean = jnp.sum(field, axis=1, keepdims=True, dtype=jnp.float32) / SAMPLE_NUMBER
    perturb = (field - state_mean).astype(jnp.bfloat16)
    pieces, state_mean, perturb = lax.optimization_barrier((pieces, state_mean, perturb))

    weights = flipped_weights(pieces)
    routed = [weights[0]] + [swap(weights[e], e) for e in range(1, 4)]
    return analysed(perturb, state_mean, routed).transpose(1, 0, 2)


def solution(mesh):
    grid = Mesh(mesh.devices.reshape(4, 2, 4, 4, 2), ("mem", "ylo", "x", "zq", "zp"))
    return on_grid(grid)


def on_grid(grid):
    reg = ("ylo", "x", "zq", "zp")
    every = ("mem",) + reg
    placed = (
        P("mem", reg, None),
        P(every, None, None),
        P(every, None),
        P(every, None),
        P(every),
        P(every, None),
        P(every),
    )
    return jax.shard_map(
        per_device, mesh=grid, in_specs=placed, out_specs=P("mem", reg, None), check_vma=False
    )
```

```python
import functools
import math

import jax
import jax.numpy as jnp
from jax import lax
from jax.experimental import pallas as pl
from jax.experimental.pallas import tpu as pltpu
from jax.sharding import Mesh
from jax.sharding import PartitionSpec as P


SAMPLE_NUMBER = 256
OB = 128
CAP = 2
PATCH_REG = 8
ITERS = 5
META = 8
ROWS = CAP * OB + META
HALF = SAMPLE_NUMBER // 2
MEMBERS = SAMPLE_NUMBER // 4
PACK = 2 * HALF + 16
GROUP = ("mem", "ylo", "x", "zp")
STEP = 8
ALONG = (0, 2, 1, 3)
TAGS = 16


def prep_kernel(
    ways, zone_smem, tally_smem, tile_smem, anom_ref, spread_ref, depart_ref, out_ref, anom_buf,
    meta_wide, counts, sems
):
    blocks = anom_ref.shape[0]
    regions = out_ref.shape[0]
    zq_ways, plane_ways, zp_ways = ways
    zq = lax.axis_index("zq")

    def load(g):
        part = pl.ds(g * STEP, STEP)
        return pltpu.make_async_copy(anom_ref.at[part], anom_buf.at[part], sems.at[g])

    for g in range(blocks // STEP):
        load(g).start()

    @pl.loop(0, regions)
    def _(r):
        counts[r] = 0

    meta_wide[...] = jnp.zeros_like(meta_wide)
    block_row = lax.broadcasted_iota(jnp.int32, (STEP, OB), 0)
    lane = lax.broadcasted_iota(jnp.int32, (STEP, OB), 1)

    @pl.loop(0, blocks // STEP)
    def _(g):
        part = pl.ds(pl.multiple_of(g * STEP, STEP), STEP)
        tally = jnp.zeros((STEP, OB), jnp.int32)
        for j in range(STEP):
            tally = jnp.where(block_row == j, tally_smem[g * STEP + j], tally)
        kept = jnp.where(lane < tally, spread_ref[part, :], 0.0)
        weighted = depart_ref[part, :] * kept
        weight_t = kept.T
        load(g).wait()
        for j in range(STEP):
            b = g * STEP + j
            region = zone_smem[b]
            rank = counts[region]
            counts[region] = rank + 1
            rest = region // zp_ways
            along = (rest % zq_ways - zq + zq_ways) % zq_ways
            mem = along % 2 * 2 + along // 2
            place = (mem * plane_ways + rest // zq_ways) * zp_ways + region % zp_ways

            scaled = anom_buf[b].astype(jnp.float32) * weight_t[:, j : j + 1]
            start = pl.multiple_of(rank * OB, OB)
            out_ref[place, pl.ds(start, OB), :] = scaled.astype(jnp.bfloat16)

            tag = jnp.full((1, OB), tile_smem[b] + 1, jnp.int32).astype(jnp.float32)
            content = jnp.concatenate([weighted[j : j + 1], tag], axis=1)
            meta_wide[place, pl.ds(rank, 1), :] = content

    out_ref[:, CAP * OB :, :] = meta_wide[...].astype(jnp.bfloat16)


def build_messages(anomalies, spread, departure, tally, tile, zone, ways):
    blocks = anomalies.shape[0]
    regions = math.prod(ways)
    scalars = pl.BlockSpec(memory_space=pltpu.SMEM)
    vectors = pl.BlockSpec(memory_space=pltpu.VMEM)
    return pl.pallas_call(
        functools.partial(prep_kernel, ways),
        out_shape=jax.ShapeDtypeStruct((regions, ROWS, SAMPLE_NUMBER), jnp.bfloat16),
        in_specs=[scalars] * 3 + [pl.BlockSpec(memory_space=pl.ANY)] + [vectors] * 2,
        out_specs=vectors,
        scratch_shapes=[
            pltpu.VMEM((blocks, OB, SAMPLE_NUMBER), jnp.bfloat16),
            pltpu.VMEM((regions, META, SAMPLE_NUMBER), jnp.float32),
            pltpu.SMEM((regions,), jnp.int32),
            pltpu.SemaphoreType.DMA((blocks // STEP,)),
        ],
        compiler_params=pltpu.CompilerParams(vmem_limit_bytes=24 << 20),
        cost_estimate=pl.CostEstimate(flops=0, bytes_accessed=1 << 23, transcendentals=0),
        name="build_messages",
    )(zone, tally, tile, anomalies, spread, departure)


def high_low(row):
    high = row.astype(jnp.bfloat16)
    return high, (row - high.astype(jnp.float32)).astype(jnp.bfloat16)


def gram_kernel(tag_ref, rows_ref, *refs):
    outs, (upper, corner, tag_vmem, tag_smem, tag_sem) = refs[:2], refs[2:]
    step, mem = pl.program_id(0), lax.axis_index("mem")
    sources = rows_ref.shape[0]

    @pl.when(step == 0)
    def _():
        weight = lax.broadcasted_iota(jnp.int32, tag_ref.shape, 1)
        weight = jnp.where(weight == 0, 1.0, jnp.where(weight == 1, TAGS, 0.0))
        codes = jnp.sum(tag_ref[...].astype(jnp.float32) * weight, axis=1)
        tag_vmem[...] = codes.astype(jnp.int32)
        tag_copy = pltpu.make_async_copy(tag_vmem, tag_smem, tag_sem)
        tag_copy.start()
        upper[...] = jnp.zeros_like(upper)
        corner[...] = jnp.zeros_like(corner)
        tag_copy.wait()

    place = lax.broadcasted_iota(jnp.int32, (META, OB), 0)
    for s in range(sources):
        meta = rows_ref[s, CAP * OB : ROWS, :OB].astype(jnp.float32)
        for i in range(CAP):
            code = tag_smem[step * sources + s, 0]
            tag = (code // TAGS if i else code % TAGS) - 1
            turned = ((tag // 2) ^ mem) * 2 + tag % 2
            tag = jnp.where(tag >= 0, turned, PATCH_REG)
            block = rows_ref[s, i * OB : (i + 1) * OB, :]
            flipped = block.T
            innovation = jnp.where(place == i, meta, 0.0).astype(jnp.bfloat16)
            left = jnp.concatenate([flipped[:HALF], innovation], axis=0)
            upper[tag] += jnp.dot(left, block, preferred_element_type=jnp.float32)
            corner[tag] += jnp.dot(
                flipped[HALF:], block[:, HALF:], preferred_element_type=jnp.float32
            )

    @pl.when(step == pl.num_programs(0) - 1)
    def _():
        row = lax.broadcasted_iota(jnp.int32, (HALF, HALF), 0)
        col = lax.broadcasted_iota(jnp.int32, (HALF, HALF), 1)
        for p in range(PATCH_REG):
            first, last = upper[p, :HALF, :HALF], corner[p]
            mixed = jnp.where(row >= col, first, last)
            diagonal = jnp.sum(jnp.where(row == col, last, 0.0), axis=0, keepdims=True)
            drive = jnp.sum(upper[p, HALF:, :], axis=0, keepdims=True)
            extra = jnp.concatenate([diagonal, drive[:, :HALF], drive[:, HALF:]], axis=0)
            high, low = high_low(extra)
            tail = jnp.concatenate(
                [
                    high.astype(jnp.float32),
                    low.astype(jnp.float32),
                    jnp.zeros((PACK - 2 * HALF - 6, HALF), jnp.float32),
                ],
                axis=0,
            )
            out = outs[p // 4].at[p // 2 % 2, p % 2]
            out[:HALF, :] = upper[p, :HALF, HALF:].astype(jnp.bfloat16)
            out[HALF : 2 * HALF, :] = mixed.astype(jnp.bfloat16)
            out[2 * HALF :, :] = tail.astype(jnp.bfloat16)


def partial_grams(messages):
    regions = messages.shape[0]
    sources = min(8, regions)
    pairs = jax.ShapeDtypeStruct((2, 2, PACK, HALF), jnp.bfloat16)
    return pl.pallas_call(
        gram_kernel,
        out_shape=[pairs] * 2,
        grid_spec=pl.GridSpec(
            grid=(regions // sources,),
            in_specs=[
                pl.BlockSpec((regions, META, OB), lambda i: (0, CAP * OB // META, 1)),
                pl.BlockSpec((sources, ROWS, SAMPLE_NUMBER), lambda i: (i, 0, 0)),
            ],
            out_specs=[pl.BlockSpec((2, 2, PACK, HALF), lambda i: (0, 0, 0, 0))] * 2,
            scratch_shapes=[
                pltpu.VMEM((PATCH_REG + 1, HALF + META, SAMPLE_NUMBER), jnp.float32),
                pltpu.VMEM((PATCH_REG + 1, HALF, HALF), jnp.float32),
                pltpu.VMEM((regions, OB), jnp.int32),
                pltpu.SMEM((regions, OB), jnp.int32),
                pltpu.SemaphoreType.DMA,
            ],
        ),
        compiler_params=pltpu.CompilerParams(vmem_limit_bytes=12 << 20),
        cost_estimate=pl.CostEstimate(flops=1 << 31, bytes_accessed=1 << 23, transcendentals=0),
        name="partial_grams",
    )(messages, messages)


def split(a):
    high = a.astype(jnp.bfloat16)
    return high, (a - high.astype(jnp.float32)).astype(jnp.bfloat16)


def product(a, b):
    left = jnp.concatenate([a[0], a[1], a[0]], axis=1)
    right = jnp.concatenate([b[0], b[0], b[1]], axis=0)
    return jnp.dot(left, right, preferred_element_type=jnp.float32)


def newton_kernel(a_ref, b_ref, c_ref, *refs):
    mem = lax.axis_index("mem")
    outs, (gram_ref, weight_ref) = refs[:4], refs[4:]
    row = lax.broadcasted_iota(jnp.int32, (HALF, HALF), 0)
    col = lax.broadcasted_iota(jnp.int32, (HALF, HALF), 1)
    row_full = lax.broadcasted_iota(jnp.int32, (SAMPLE_NUMBER, SAMPLE_NUMBER), 0)
    col_full = lax.broadcasted_iota(jnp.int32, (SAMPLE_NUMBER, SAMPLE_NUMBER), 1)
    identity = jnp.where(row_full == col_full, 1.0, 0.0)
    drives, frobs, roots, inverses, steps = [], [], [], [], []
    for p in range(2):
        parts = (a_ref[0, p], b_ref[0, p], c_ref[0, p], c_ref[1, p])
        total = sum(part.astype(jnp.float32) for part in parts)
        cross, mixed, tail = total[:HALF], total[HALF : 2 * HALF], total[2 * HALF :]
        extra = tail[0:3] + tail[3:6]
        turned = mixed.T
        gram_ref[p, :HALF, :HALF] = jnp.where(row >= col, mixed, turned)
        gram_ref[p, :HALF, HALF:] = cross
        gram_ref[p, HALF:, :HALF] = cross.T
        gram_ref[p, HALF:, HALF:] = jnp.where(
            row == col, extra[0:1], jnp.where(row < col, mixed, turned)
        )
        drives.append(jnp.concatenate([extra[1:2], extra[2:3]], axis=1))
        gram = gram_ref[p] + (SAMPLE_NUMBER - 1.0) * identity
        squares = jnp.sum(jnp.sum(gram * gram, axis=0, keepdims=True), axis=1, keepdims=True)
        frobs.append(jnp.sqrt(squares))
        roots.append(gram / frobs[p])
        steps.append(1.5 * identity - 0.5 * roots[p])
        inverses.append(steps[p])
    for _ in range(1, ITERS):
        step_parts = [split(step) for step in steps]
        roots = [product(split(root), step) for root, step in zip(roots, step_parts)]
        inverse_parts = [split(inverse) for inverse in inverses]
        steps = [
            1.5 * identity - 0.5 * product(inverse, split(root))
            for inverse, root in zip(inverse_parts, roots)
        ]
        inverses = [
            product(split(step), inverse) for step, inverse in zip(steps, inverse_parts)
        ]
    for p in range(2):
        inv_root = inverses[p] / jnp.sqrt(frobs[p])
        once = jnp.sum(inv_root * drives[p], axis=1, keepdims=True)
        mean_weight = jnp.sum(inv_root * once, axis=0, keepdims=True)
        weight_ref[p] = math.sqrt(SAMPLE_NUMBER - 1.0) * inv_root + mean_weight
        for e in range(4):
            goal = mem ^ e
            part = weight_ref[p, pl.ds(pl.multiple_of(goal * MEMBERS, MEMBERS), MEMBERS), :]
            low, high = part[:, :HALF], part[:, HALF:]
            low, high = jnp.where(goal >= 2, high, low), jnp.where(goal >= 2, low, high)
            for i, side in enumerate((low, high)):
                side = jnp.where(goal % 2 == 1, pltpu.roll(side, MEMBERS, 1), side)
                outs[e][p, :, i * HALF : (i + 1) * HALF] = side.astype(jnp.bfloat16)


def flipped_weights(pieces):
    piece = jax.ShapeDtypeStruct((2, MEMBERS, SAMPLE_NUMBER), jnp.bfloat16)
    return pl.pallas_call(
        newton_kernel,
        out_shape=[piece] * 4,
        scratch_shapes=[
            pltpu.VMEM((2, SAMPLE_NUMBER, SAMPLE_NUMBER), jnp.float32),
            pltpu.VMEM((2, SAMPLE_NUMBER, SAMPLE_NUMBER), jnp.float32),
        ],
        compiler_params=pltpu.CompilerParams(vmem_limit_bytes=16 << 20),
        name="weights",
    )(*pieces)


def analysis_kernel(perturb_ref, mean_ref, *refs):
    routed, out_ref = refs[:4], refs[4]
    mem = lax.axis_index("mem")
    for e in range(4):
        for i in range(2):
            p = (mem ^ e) * 2 + i
            update = jnp.dot(routed[e][i], perturb_ref[p], preferred_element_type=jnp.float32)
            out_ref[p] = (mean_ref[p] + update).astype(jnp.bfloat16)


def analysed(perturb, state_mean, routed):
    return pl.pallas_call(
        analysis_kernel,
        out_shape=jax.ShapeDtypeStruct(
            (PATCH_REG, MEMBERS, perturb.shape[2]), jnp.bfloat16
        ),
        compiler_params=pltpu.CompilerParams(vmem_limit_bytes=12 << 20),
        name="analysed",
    )(perturb, state_mean, *routed)


def swap(x, bit):
    return lax.ppermute(x, "mem", [(j, j ^ bit) for j in range(4)])


def to_owner(x, bit):
    pairs = [(m * 4 + z, (m ^ bit) * 4 + (z + ALONG[m]) % 4) for m in range(4) for z in range(4)]
    return lax.ppermute(x, ("mem", "zq"), pairs)


def per_device(prior, anomalies, spread, departure, tally, zone, tile):
    ways = {a: lax.axis_size(a) for a in ("ylo", "x", "zq", "zp")}
    in_hbm = lambda x: pltpu.with_memory_space_constraint(x, pltpu.HBM)
    far = swap(prior.reshape(-1, prior.shape[2]), 2)
    messages = build_messages(
        *(in_hbm(x) for x in (anomalies, spread, departure, tally, tile, zone[:, 0])),
        (ways["zq"], ways["ylo"] * ways["x"], ways["zp"]),
    )
    arrived = lax.all_to_all(messages, GROUP, split_axis=0, concat_axis=0, tiled=True)
    arrived, prior = lax.optimization_barrier((arrived, prior))
    near = swap(prior, 1)

    pieces = partial_grams(arrived)
    same, other = to_owner(pieces[0], 0), to_owner(pieces[1], 2)

    farther = swap(far, 1)
    far, farther = (x.reshape(prior.shape) for x in (far, farther))
    field = jnp.concatenate([prior, near, far, farther], axis=0).transpose(1, 0, 2)
    state_mean = jnp.sum(field, axis=1, keepdims=True, dtype=jnp.float32) / SAMPLE_NUMBER
    perturb = (field - state_mean).astype(jnp.bfloat16)
    same, other, state_mean, perturb = lax.optimization_barrier(
        (same, other, state_mean, perturb)
    )
    crossed = swap(jnp.stack([same[1], other[1]]), 1)
    weights = flipped_weights((same, other, crossed))
    routed = [weights[0]] + [swap(weights[e], e) for e in range(1, 4)]
    return analysed(perturb, state_mean, routed).transpose(1, 0, 2)


def solution(mesh):
    grid = Mesh(mesh.devices.reshape(4, 2, 4, 4, 2), ("mem", "ylo", "x", "zq", "zp"))
    return on_grid(grid)


def on_grid(grid):
    reg = ("ylo", "x", "zq", "zp")
    every = ("mem",) + reg
    placed = (
        P("mem", reg, None),
        P(every, None, None),
        P(every, None),
        P(every, None),
        P(every),
        P(every, None),
        P(every),
    )
    return jax.shard_map(
        per_device, mesh=grid, in_specs=placed, out_specs=P("mem", reg, None), check_vma=False
    )
```

```python
import functools
import itertools
import math

import jax
import jax.numpy as jnp
from jax import lax
from jax.experimental import pallas as pl
from jax.experimental.pallas import tpu as pltpu
from jax.sharding import Mesh
from jax.sharding import PartitionSpec as P


SAMPLE_NUMBER = 256
OB = 128
CAP = 2
PATCH_REG = 8
ITERS = 5
META = 8
ROWS = CAP * OB + META
HALF = SAMPLE_NUMBER // 2
MEMBERS = SAMPLE_NUMBER // 4
PACK = 2 * HALF + 16
GROUP = ("mem", "ylo", "x", "zp")
STEP = 8
ALONG = (0, 2, 1, 3)
TAGS = 16


def prep_kernel(
    ways, zone_smem, tally_smem, tile_smem, anom_ref, spread_ref, depart_ref, out_ref, anom_buf,
    meta_wide, counts, sems
):
    blocks = anom_ref.shape[0]
    regions = out_ref.shape[0]
    ylo_ways, x_ways, zq_ways, zp_ways = ways
    zq = lax.axis_index("zq")

    def load(g):
        part = pl.ds(g * STEP, STEP)
        return pltpu.make_async_copy(anom_ref.at[part], anom_buf.at[part], sems.at[g])

    for g in range(blocks // STEP):
        load(g).start()

    @pl.loop(0, regions)
    def _(r):
        counts[r] = 0

    meta_wide[...] = jnp.zeros_like(meta_wide)
    block_row = lax.broadcasted_iota(jnp.int32, (STEP, OB), 0)
    lane = lax.broadcasted_iota(jnp.int32, (STEP, OB), 1)

    @pl.loop(0, blocks // STEP)
    def _(g):
        part = pl.ds(pl.multiple_of(g * STEP, STEP), STEP)
        tally = jnp.zeros((STEP, OB), jnp.int32)
        for j in range(STEP):
            tally = jnp.where(block_row == j, tally_smem[g * STEP + j], tally)
        kept = jnp.where(lane < tally, spread_ref[part, :], 0.0)
        weighted = depart_ref[part, :] * kept
        weight_t = kept.T
        load(g).wait()
        for j in range(STEP):
            b = g * STEP + j
            region = zone_smem[b]
            rank = counts[region]
            counts[region] = rank + 1
            rest = region // zp_ways
            along = (rest % zq_ways - zq + zq_ways) % zq_ways
            mem = along % 2 * 2 + along // 2
            plane = (rest // zq_ways + x_ways) % (ylo_ways * x_ways)
            zp = region % zp_ways
            zp = jnp.where(mem == 1, zp_ways - 1 - zp, zp)
            place = (mem * ylo_ways * x_ways + plane) * zp_ways + zp

            scaled = anom_buf[b].astype(jnp.float32) * weight_t[:, j : j + 1]
            start = pl.multiple_of(rank * OB, OB)
            out_ref[place, pl.ds(start, OB), :] = scaled.astype(jnp.bfloat16)

            tag = jnp.full((1, OB), tile_smem[b] + 1, jnp.int32).astype(jnp.float32)
            content = jnp.concatenate([weighted[j : j + 1], tag], axis=1)
            meta_wide[place, pl.ds(rank, 1), :] = content

    out_ref[:, CAP * OB :, :] = meta_wide[...].astype(jnp.bfloat16)


def build_messages(anomalies, spread, departure, tally, tile, zone, ways):
    blocks = anomalies.shape[0]
    regions = math.prod(ways)
    scalars = pl.BlockSpec(memory_space=pltpu.SMEM)
    vectors = pl.BlockSpec(memory_space=pltpu.VMEM)
    return pl.pallas_call(
        functools.partial(prep_kernel, ways),
        out_shape=jax.ShapeDtypeStruct((regions, ROWS, SAMPLE_NUMBER), jnp.bfloat16),
        in_specs=[scalars] * 3 + [pl.BlockSpec(memory_space=pl.ANY)] + [vectors] * 2,
        out_specs=vectors,
        scratch_shapes=[
            pltpu.VMEM((blocks, OB, SAMPLE_NUMBER), jnp.bfloat16),
            pltpu.VMEM((regions, META, SAMPLE_NUMBER), jnp.float32),
            pltpu.SMEM((regions,), jnp.int32),
            pltpu.SemaphoreType.DMA((blocks // STEP,)),
        ],
        compiler_params=pltpu.CompilerParams(vmem_limit_bytes=24 << 20),
        cost_estimate=pl.CostEstimate(flops=0, bytes_accessed=1 << 23, transcendentals=0),
        name="build_messages",
    )(zone, tally, tile, anomalies, spread, departure)


def high_low(row):
    high = row.astype(jnp.bfloat16)
    return high, (row - high.astype(jnp.float32)).astype(jnp.bfloat16)


def gram_kernel(tag_ref, rows_ref, *refs):
    outs, (upper, corner, tag_vmem, tag_smem, tag_sem) = refs[:2], refs[2:]
    step, mem = pl.program_id(0), lax.axis_index("mem")
    sources = rows_ref.shape[0]

    @pl.when(step == 0)
    def _():
        weight = lax.broadcasted_iota(jnp.int32, tag_ref.shape, 1)
        weight = jnp.where(weight == 0, 1.0, jnp.where(weight == 1, TAGS, 0.0))
        codes = jnp.sum(tag_ref[...].astype(jnp.float32) * weight, axis=1)
        tag_vmem[...] = codes.astype(jnp.int32)
        tag_copy = pltpu.make_async_copy(tag_vmem, tag_smem, tag_sem)
        tag_copy.start()
        upper[...] = jnp.zeros_like(upper)
        corner[...] = jnp.zeros_like(corner)
        tag_copy.wait()

    place = lax.broadcasted_iota(jnp.int32, (META, OB), 0)
    for s in range(sources):
        meta = rows_ref[s, CAP * OB : ROWS, :OB].astype(jnp.float32)
        for i in range(CAP):
            code = tag_smem[step * sources + s, 0]
            tag = (code // TAGS if i else code % TAGS) - 1
            turned = ((tag // 2) ^ mem) * 2 + tag % 2
            tag = jnp.where(tag >= 0, turned, PATCH_REG)
            block = rows_ref[s, i * OB : (i + 1) * OB, :]
            flipped = block.T
            innovation = jnp.where(place == i, meta, 0.0).astype(jnp.bfloat16)
            left = jnp.concatenate([flipped[:HALF], innovation], axis=0)
            upper[tag] += jnp.dot(left, block, preferred_element_type=jnp.float32)
            corner[tag] += jnp.dot(
                flipped[HALF:], block[:, HALF:], preferred_element_type=jnp.float32
            )

    @pl.when(step == pl.num_programs(0) - 1)
    def _():
        row = lax.broadcasted_iota(jnp.int32, (HALF, HALF), 0)
        col = lax.broadcasted_iota(jnp.int32, (HALF, HALF), 1)
        for p in range(PATCH_REG):
            first, last = upper[p, :HALF, :HALF], corner[p]
            mixed = jnp.where(row >= col, first, last)
            diagonal = jnp.sum(jnp.where(row == col, last, 0.0), axis=0, keepdims=True)
            drive = jnp.sum(upper[p, HALF:, :], axis=0, keepdims=True)
            extra = jnp.concatenate([diagonal, drive[:, :HALF], drive[:, HALF:]], axis=0)
            high, low = high_low(extra)
            tail = jnp.concatenate(
                [
                    high.astype(jnp.float32),
                    low.astype(jnp.float32),
                    jnp.zeros((PACK - 2 * HALF - 6, HALF), jnp.float32),
                ],
                axis=0,
            )
            out = outs[p // 4].at[p // 2 % 2, p % 2]
            out[:HALF, :] = upper[p, :HALF, HALF:].astype(jnp.bfloat16)
            out[HALF : 2 * HALF, :] = mixed.astype(jnp.bfloat16)
            out[2 * HALF :, :] = tail.astype(jnp.bfloat16)


def partial_grams(messages):
    regions = messages.shape[0]
    sources = min(8, regions)
    pairs = jax.ShapeDtypeStruct((2, 2, PACK, HALF), jnp.bfloat16)
    return pl.pallas_call(
        gram_kernel,
        out_shape=[pairs] * 2,
        grid_spec=pl.GridSpec(
            grid=(regions // sources,),
            in_specs=[
                pl.BlockSpec((regions, META, OB), lambda i: (0, CAP * OB // META, 1)),
                pl.BlockSpec((sources, ROWS, SAMPLE_NUMBER), lambda i: (i, 0, 0)),
            ],
            out_specs=[pl.BlockSpec((2, 2, PACK, HALF), lambda i: (0, 0, 0, 0))] * 2,
            scratch_shapes=[
                pltpu.VMEM((PATCH_REG + 1, HALF + META, SAMPLE_NUMBER), jnp.float32),
                pltpu.VMEM((PATCH_REG + 1, HALF, HALF), jnp.float32),
                pltpu.VMEM((regions, OB), jnp.int32),
                pltpu.SMEM((regions, OB), jnp.int32),
                pltpu.SemaphoreType.DMA,
            ],
        ),
        compiler_params=pltpu.CompilerParams(vmem_limit_bytes=12 << 20),
        cost_estimate=pl.CostEstimate(flops=1 << 31, bytes_accessed=1 << 23, transcendentals=0),
        name="partial_grams",
    )(messages, messages)


def split(a):
    high = a.astype(jnp.bfloat16)
    return high, (a - high.astype(jnp.float32)).astype(jnp.bfloat16)


def product(a, b):
    left = jnp.concatenate([a[0], a[1], a[0]], axis=1)
    right = jnp.concatenate([b[0], b[0], b[1]], axis=0)
    return jnp.dot(left, right, preferred_element_type=jnp.float32)


def newton_kernel(a_ref, b_ref, c_ref, *refs):
    mem = lax.axis_index("mem")
    outs, (gram_ref, weight_ref) = refs[:4], refs[4:]
    row = lax.broadcasted_iota(jnp.int32, (HALF, HALF), 0)
    col = lax.broadcasted_iota(jnp.int32, (HALF, HALF), 1)
    row_full = lax.broadcasted_iota(jnp.int32, (SAMPLE_NUMBER, SAMPLE_NUMBER), 0)
    col_full = lax.broadcasted_iota(jnp.int32, (SAMPLE_NUMBER, SAMPLE_NUMBER), 1)
    identity = jnp.where(row_full == col_full, 1.0, 0.0)
    drives, frobs, roots, inverses, steps = [], [], [], [], []
    for p in range(2):
        parts = (a_ref[0, p], b_ref[0, p], c_ref[0, p], c_ref[1, p])
        total = sum(part.astype(jnp.float32) for part in parts)
        cross, mixed, tail = total[:HALF], total[HALF : 2 * HALF], total[2 * HALF :]
        extra = tail[0:3] + tail[3:6]
        turned = mixed.T
        gram_ref[p, :HALF, :HALF] = jnp.where(row >= col, mixed, turned)
        gram_ref[p, :HALF, HALF:] = cross
        gram_ref[p, HALF:, :HALF] = cross.T
        gram_ref[p, HALF:, HALF:] = jnp.where(
            row == col, extra[0:1], jnp.where(row < col, mixed, turned)
        )
        drives.append(jnp.concatenate([extra[1:2], extra[2:3]], axis=1))
        gram = gram_ref[p] + (SAMPLE_NUMBER - 1.0) * identity
        squares = jnp.sum(jnp.sum(gram * gram, axis=0, keepdims=True), axis=1, keepdims=True)
        frobs.append(jnp.sqrt(squares))
        roots.append(gram / frobs[p])
        steps.append(1.5 * identity - 0.5 * roots[p])
        inverses.append(steps[p])
    for _ in range(1, ITERS):
        step_parts = [split(step) for step in steps]
        roots = [product(split(root), step) for root, step in zip(roots, step_parts)]
        inverse_parts = [split(inverse) for inverse in inverses]
        steps = [
            1.5 * identity - 0.5 * product(inverse, split(root))
            for inverse, root in zip(inverse_parts, roots)
        ]
        inverses = [
            product(split(step), inverse) for step, inverse in zip(steps, inverse_parts)
        ]
    for p in range(2):
        inv_root = inverses[p] / jnp.sqrt(frobs[p])
        once = jnp.sum(inv_root * drives[p], axis=1, keepdims=True)
        mean_weight = jnp.sum(inv_root * once, axis=0, keepdims=True)
        weight_ref[p] = math.sqrt(SAMPLE_NUMBER - 1.0) * inv_root + mean_weight
        for e in range(4):
            goal = mem ^ e
            part = weight_ref[p, pl.ds(pl.multiple_of(goal * MEMBERS, MEMBERS), MEMBERS), :]
            low, high = part[:, :HALF], part[:, HALF:]
            low, high = jnp.where(goal >= 2, high, low), jnp.where(goal >= 2, low, high)
            for i, side in enumerate((low, high)):
                side = jnp.where(goal % 2 == 1, pltpu.roll(side, MEMBERS, 1), side)
                outs[e][p, :, i * HALF : (i + 1) * HALF] = side.astype(jnp.bfloat16)


def flipped_weights(pieces):
    piece = jax.ShapeDtypeStruct((2, MEMBERS, SAMPLE_NUMBER), jnp.bfloat16)
    return pl.pallas_call(
        newton_kernel,
        out_shape=[piece] * 4,
        scratch_shapes=[
            pltpu.VMEM((2, SAMPLE_NUMBER, SAMPLE_NUMBER), jnp.float32),
            pltpu.VMEM((2, SAMPLE_NUMBER, SAMPLE_NUMBER), jnp.float32),
        ],
        compiler_params=pltpu.CompilerParams(vmem_limit_bytes=16 << 20),
        name="weights",
    )(*pieces)


def analysis_kernel(perturb_ref, mean_ref, *refs):
    routed, out_ref = refs[:4], refs[4]
    mem = lax.axis_index("mem")
    for e in range(4):
        for i in range(2):
            p = (mem ^ e) * 2 + i
            update = jnp.dot(routed[e][i], perturb_ref[p], preferred_element_type=jnp.float32)
            out_ref[p] = (mean_ref[p] + update).astype(jnp.bfloat16)


def analysed(perturb, state_mean, routed):
    return pl.pallas_call(
        analysis_kernel,
        out_shape=jax.ShapeDtypeStruct(
            (PATCH_REG, MEMBERS, perturb.shape[2]), jnp.bfloat16
        ),
        compiler_params=pltpu.CompilerParams(vmem_limit_bytes=12 << 20),
        name="analysed",
    )(perturb, state_mean, *routed)


def swap(x, bit):
    return lax.ppermute(x, "mem", [(j, j ^ bit) for j in range(4)])


def to_owner(x, bit):
    axes = ("mem", "ylo", "zq", "zp")
    sizes = [lax.axis_size(a) for a in axes]
    pairs = []
    for m, y, z, h in itertools.product(*(range(n) for n in sizes)):
        goal = (m ^ bit, (y + 1) % sizes[1], (z + ALONG[m]) % sizes[2], sizes[3] - 1 - h if m == 1 else h)
        flat = [((a * sizes[1] + b) * sizes[2] + c) * sizes[3] + d for a, b, c, d in ((m, y, z, h), goal)]
        pairs.append(tuple(flat))
    return lax.ppermute(x, axes, pairs)


def per_device(prior, anomalies, spread, departure, tally, zone, tile):
    ways = {a: lax.axis_size(a) for a in ("ylo", "x", "zq", "zp")}
    in_hbm = lambda x: pltpu.with_memory_space_constraint(x, pltpu.HBM)
    far = swap(prior.reshape(-1, prior.shape[2]), 2)
    messages = build_messages(
        *(in_hbm(x) for x in (anomalies, spread, departure, tally, tile, zone[:, 0])),
        tuple(ways.values()),
    )
    arrived = lax.all_to_all(messages, GROUP, split_axis=0, concat_axis=0, tiled=True)
    arrived, prior = lax.optimization_barrier((arrived, prior))
    near = swap(prior, 1)

    pieces = partial_grams(arrived)
    same, other = to_owner(pieces[0], 0), to_owner(pieces[1], 2)

    farther = swap(far, 1)
    far, farther = (x.reshape(prior.shape) for x in (far, farther))
    field = jnp.concatenate([prior, near, far, farther], axis=0).transpose(1, 0, 2)
    state_mean = jnp.sum(field, axis=1, keepdims=True, dtype=jnp.float32) / SAMPLE_NUMBER
    perturb = (field - state_mean).astype(jnp.bfloat16)
    same, other, state_mean, perturb = lax.optimization_barrier(
        (same, other, state_mean, perturb)
    )
    crossed = swap(jnp.stack([same[1], other[1]]), 1)
    weights = flipped_weights((same, other, crossed))
    routed = [weights[0]] + [swap(weights[e], e) for e in range(1, 4)]
    return analysed(perturb, state_mean, routed).transpose(1, 0, 2)


def solution(mesh):
    grid = Mesh(mesh.devices.reshape(4, 2, 4, 4, 2), ("mem", "ylo", "x", "zq", "zp"))
    return on_grid(grid)


def on_grid(grid):
    reg = ("ylo", "x", "zq", "zp")
    every = ("mem",) + reg
    placed = (
        P("mem", reg, None),
        P(every, None, None),
        P(every, None),
        P(every, None),
        P(every),
        P(every, None),
        P(every),
    )
    return jax.shard_map(
        per_device, mesh=grid, in_specs=placed, out_specs=P("mem", reg, None), check_vma=False
    )
```

```python
import functools
import itertools
import math

import jax
import jax.numpy as jnp
from jax import lax
from jax.experimental import pallas as pl
from jax.experimental.pallas import tpu as pltpu
from jax.sharding import Mesh
from jax.sharding import PartitionSpec as P


SAMPLE_NUMBER = 256
OB = 128
CAP = 2
PATCH_REG = 8
ITERS = 5
META = 8
ROWS = CAP * OB + META
HALF = SAMPLE_NUMBER // 2
MEMBERS = SAMPLE_NUMBER // 4
PACK = 2 * HALF + 16
GROUP = ("mem", "ylo", "x", "zp")
STEP = 8
ALONG = (0, 2, 1, 3)
TAGS = 16


def prep_kernel(
    ways, zone_smem, tally_smem, tile_smem, anom_ref, spread_ref, depart_ref, out_ref, anom_buf,
    meta_wide, counts, sems
):
    blocks = anom_ref.shape[0]
    regions = out_ref.shape[0]
    ylo_ways, x_ways, zq_ways, zp_ways = ways
    zq = lax.axis_index("zq")

    def load(g):
        part = pl.ds(g * STEP, STEP)
        return pltpu.make_async_copy(anom_ref.at[part], anom_buf.at[part], sems.at[g])

    for g in range(blocks // STEP):
        load(g).start()

    @pl.loop(0, regions)
    def _(r):
        counts[r] = 0

    meta_wide[...] = jnp.zeros_like(meta_wide)
    block_row = lax.broadcasted_iota(jnp.int32, (STEP, OB), 0)
    lane = lax.broadcasted_iota(jnp.int32, (STEP, OB), 1)

    @pl.loop(0, blocks // STEP)
    def _(g):
        part = pl.ds(pl.multiple_of(g * STEP, STEP), STEP)
        tally = jnp.zeros((STEP, OB), jnp.int32)
        for j in range(STEP):
            tally = jnp.where(block_row == j, tally_smem[g * STEP + j], tally)
        kept = jnp.where(lane < tally, spread_ref[part, :], 0.0)
        weighted = depart_ref[part, :] * kept
        weight_t = kept.T
        load(g).wait()
        for j in range(STEP):
            b = g * STEP + j
            region = zone_smem[b]
            rank = counts[region]
            counts[region] = rank + 1
            rest = region // zp_ways
            along = (rest % zq_ways - zq + zq_ways) % zq_ways
            mem = along % 2 * 2 + along // 2
            plane = (rest // zq_ways + x_ways) % (ylo_ways * x_ways)
            zp = region % zp_ways
            zp = jnp.where(mem == 1, zp_ways - 1 - zp, zp)
            place = (mem * ylo_ways * x_ways + plane) * zp_ways + zp

            scaled = anom_buf[b].astype(jnp.float32) * weight_t[:, j : j + 1]
            start = pl.multiple_of(rank * OB, OB)
            out_ref[place, pl.ds(start, OB), :] = scaled.astype(jnp.bfloat16)

            tag = jnp.full((1, OB), tile_smem[b] + 1, jnp.int32).astype(jnp.float32)
            content = jnp.concatenate([weighted[j : j + 1], tag], axis=1)
            meta_wide[place, pl.ds(rank, 1), :] = content

    out_ref[:, CAP * OB :, :] = meta_wide[...].astype(jnp.bfloat16)


def build_messages(anomalies, spread, departure, tally, tile, zone, ways):
    blocks = anomalies.shape[0]
    regions = math.prod(ways)
    scalars = pl.BlockSpec(memory_space=pltpu.SMEM)
    vectors = pl.BlockSpec(memory_space=pltpu.VMEM)
    return pl.pallas_call(
        functools.partial(prep_kernel, ways),
        out_shape=jax.ShapeDtypeStruct((regions, ROWS, SAMPLE_NUMBER), jnp.bfloat16),
        in_specs=[scalars] * 3 + [pl.BlockSpec(memory_space=pl.ANY)] + [vectors] * 2,
        out_specs=vectors,
        scratch_shapes=[
            pltpu.VMEM((blocks, OB, SAMPLE_NUMBER), jnp.bfloat16),
            pltpu.VMEM((regions, META, SAMPLE_NUMBER), jnp.float32),
            pltpu.SMEM((regions,), jnp.int32),
            pltpu.SemaphoreType.DMA((blocks // STEP,)),
        ],
        compiler_params=pltpu.CompilerParams(vmem_limit_bytes=24 << 20),
        cost_estimate=pl.CostEstimate(flops=0, bytes_accessed=1 << 23, transcendentals=0),
        name="build_messages",
    )(zone, tally, tile, anomalies, spread, departure)


def high_low(row):
    high = row.astype(jnp.bfloat16)
    return high, (row - high.astype(jnp.float32)).astype(jnp.bfloat16)


def gram_kernel(tag_ref, rows_ref, *refs):
    outs, (upper, corner, tag_vmem, tag_smem, tag_sem) = refs[:2], refs[2:]
    step, mem = pl.program_id(0), lax.axis_index("mem")
    sources = rows_ref.shape[0]

    @pl.when(step == 0)
    def _():
        weight = lax.broadcasted_iota(jnp.int32, tag_ref.shape, 1)
        weight = jnp.where(weight == 0, 1.0, jnp.where(weight == 1, TAGS, 0.0))
        codes = jnp.sum(tag_ref[...].astype(jnp.float32) * weight, axis=1)
        tag_vmem[...] = codes.astype(jnp.int32)
        tag_copy = pltpu.make_async_copy(tag_vmem, tag_smem, tag_sem)
        tag_copy.start()
        upper[...] = jnp.zeros_like(upper)
        corner[...] = jnp.zeros_like(corner)
        tag_copy.wait()

    place = lax.broadcasted_iota(jnp.int32, (META, OB), 0)
    for s in range(sources):
        meta = rows_ref[s, CAP * OB : ROWS, :OB].astype(jnp.float32)
        for i in range(CAP):
            code = tag_smem[step * sources + s, 0]
            tag = (code // TAGS if i else code % TAGS) - 1
            turned = ((tag // 2) ^ mem) * 2 + tag % 2
            tag = jnp.where(tag >= 0, turned, PATCH_REG)
            block = rows_ref[s, i * OB : (i + 1) * OB, :]
            flipped = block.T
            innovation = jnp.where(place == i, meta, 0.0).astype(jnp.bfloat16)
            left = jnp.concatenate([flipped[:HALF], innovation], axis=0)
            upper[tag] += jnp.dot(left, block, preferred_element_type=jnp.float32)
            corner[tag] += jnp.dot(
                flipped[HALF:], block[:, HALF:], preferred_element_type=jnp.float32
            )

    @pl.when(step == pl.num_programs(0) - 1)
    def _():
        row = lax.broadcasted_iota(jnp.int32, (HALF, HALF), 0)
        col = lax.broadcasted_iota(jnp.int32, (HALF, HALF), 1)
        for p in range(PATCH_REG):
            first, last = upper[p, :HALF, :HALF], corner[p]
            mixed = jnp.where(row >= col, first, last)
            diagonal = jnp.sum(jnp.where(row == col, last, 0.0), axis=0, keepdims=True)
            drive = jnp.sum(upper[p, HALF:, :], axis=0, keepdims=True)
            extra = jnp.concatenate([diagonal, drive[:, :HALF], drive[:, HALF:]], axis=0)
            high, low = high_low(extra)
            tail = jnp.concatenate(
                [
                    high.astype(jnp.float32),
                    low.astype(jnp.float32),
                    jnp.zeros((PACK - 2 * HALF - 6, HALF), jnp.float32),
                ],
                axis=0,
            )
            out = outs[p // 4].at[p // 2 % 2, p % 2]
            out[:HALF, :] = upper[p, :HALF, HALF:].astype(jnp.bfloat16)
            out[HALF : 2 * HALF, :] = mixed.astype(jnp.bfloat16)
            out[2 * HALF :, :] = tail.astype(jnp.bfloat16)


def partial_grams(messages):
    regions = messages.shape[0]
    sources = min(8, regions)
    pairs = jax.ShapeDtypeStruct((2, 2, PACK, HALF), jnp.bfloat16)
    return pl.pallas_call(
        gram_kernel,
        out_shape=[pairs] * 2,
        grid_spec=pl.GridSpec(
            grid=(regions // sources,),
            in_specs=[
                pl.BlockSpec((regions, META, OB), lambda i: (0, CAP * OB // META, 1)),
                pl.BlockSpec((sources, ROWS, SAMPLE_NUMBER), lambda i: (i, 0, 0)),
            ],
            out_specs=[pl.BlockSpec((2, 2, PACK, HALF), lambda i: (0, 0, 0, 0))] * 2,
            scratch_shapes=[
                pltpu.VMEM((PATCH_REG + 1, HALF + META, SAMPLE_NUMBER), jnp.float32),
                pltpu.VMEM((PATCH_REG + 1, HALF, HALF), jnp.float32),
                pltpu.VMEM((regions, OB), jnp.int32),
                pltpu.SMEM((regions, OB), jnp.int32),
                pltpu.SemaphoreType.DMA,
            ],
        ),
        compiler_params=pltpu.CompilerParams(vmem_limit_bytes=12 << 20),
        cost_estimate=pl.CostEstimate(flops=1 << 31, bytes_accessed=1 << 23, transcendentals=0),
        name="partial_grams",
    )(messages, messages)


def split(a):
    high = a.astype(jnp.bfloat16)
    return high, (a - high.astype(jnp.float32)).astype(jnp.bfloat16)


def product(a, b):
    left = jnp.concatenate([a[0], a[1], a[0]], axis=1)
    right = jnp.concatenate([b[0], b[0], b[1]], axis=0)
    return jnp.dot(left, right, preferred_element_type=jnp.float32)


def newton_kernel(a_ref, b_ref, c_ref, d_ref, *refs):
    mem = lax.axis_index("mem")
    outs, (gram_ref, weight_ref) = refs[:4], refs[4:]
    row = lax.broadcasted_iota(jnp.int32, (HALF, HALF), 0)
    col = lax.broadcasted_iota(jnp.int32, (HALF, HALF), 1)
    row_full = lax.broadcasted_iota(jnp.int32, (SAMPLE_NUMBER, SAMPLE_NUMBER), 0)
    col_full = lax.broadcasted_iota(jnp.int32, (SAMPLE_NUMBER, SAMPLE_NUMBER), 1)
    identity = jnp.where(row_full == col_full, 1.0, 0.0)
    drives, frobs, roots, inverses, steps = [], [], [], [], []
    for p in range(2):
        parts = (a_ref[0, p], b_ref[0, p], c_ref[p], d_ref[p])
        total = sum(part.astype(jnp.float32) for part in parts)
        cross, mixed, tail = total[:HALF], total[HALF : 2 * HALF], total[2 * HALF :]
        extra = tail[0:3] + tail[3:6]
        turned = mixed.T
        gram_ref[p, :HALF, :HALF] = jnp.where(row >= col, mixed, turned)
        gram_ref[p, :HALF, HALF:] = cross
        gram_ref[p, HALF:, :HALF] = cross.T
        gram_ref[p, HALF:, HALF:] = jnp.where(
            row == col, extra[0:1], jnp.where(row < col, mixed, turned)
        )
        drives.append(jnp.concatenate([extra[1:2], extra[2:3]], axis=1))
        gram = gram_ref[p] + (SAMPLE_NUMBER - 1.0) * identity
        squares = jnp.sum(jnp.sum(gram * gram, axis=0, keepdims=True), axis=1, keepdims=True)
        frobs.append(jnp.sqrt(squares))
        roots.append(gram / frobs[p])
        steps.append(1.5 * identity - 0.5 * roots[p])
        inverses.append(steps[p])
    for _ in range(1, ITERS):
        step_parts = [split(step) for step in steps]
        roots = [product(split(root), step) for root, step in zip(roots, step_parts)]
        inverse_parts = [split(inverse) for inverse in inverses]
        steps = [
            1.5 * identity - 0.5 * product(inverse, split(root))
            for inverse, root in zip(inverse_parts, roots)
        ]
        inverses = [
            product(split(step), inverse) for step, inverse in zip(steps, inverse_parts)
        ]
    for p in range(2):
        inv_root = inverses[p] / jnp.sqrt(frobs[p])
        once = jnp.sum(inv_root * drives[p], axis=1, keepdims=True)
        mean_weight = jnp.sum(inv_root * once, axis=0, keepdims=True)
        weight_ref[p] = math.sqrt(SAMPLE_NUMBER - 1.0) * inv_root + mean_weight
        for e in range(4):
            goal = mem ^ e
            part = weight_ref[p, pl.ds(pl.multiple_of(goal * MEMBERS, MEMBERS), MEMBERS), :]
            low, high = part[:, :HALF], part[:, HALF:]
            low, high = jnp.where(goal >= 2, high, low), jnp.where(goal >= 2, low, high)
            for i, side in enumerate((low, high)):
                side = jnp.where(goal % 2 == 1, pltpu.roll(side, MEMBERS, 1), side)
                outs[e][p, :, i * HALF : (i + 1) * HALF] = side.astype(jnp.bfloat16)


def flipped_weights(pieces):
    piece = jax.ShapeDtypeStruct((2, MEMBERS, SAMPLE_NUMBER), jnp.bfloat16)
    return pl.pallas_call(
        newton_kernel,
        out_shape=[piece] * 4,
        scratch_shapes=[
            pltpu.VMEM((2, SAMPLE_NUMBER, SAMPLE_NUMBER), jnp.float32),
            pltpu.VMEM((2, SAMPLE_NUMBER, SAMPLE_NUMBER), jnp.float32),
        ],
        compiler_params=pltpu.CompilerParams(vmem_limit_bytes=16 << 20),
        name="weights",
    )(*pieces)


def analysis_kernel(perturb_ref, mean_ref, *refs):
    routed, out_ref = refs[:4], refs[4]
    mem = lax.axis_index("mem")
    for e in range(4):
        for i in range(2):
            p = (mem ^ e) * 2 + i
            update = jnp.dot(routed[e][i], perturb_ref[p], preferred_element_type=jnp.float32)
            out_ref[p] = (mean_ref[p] + update).astype(jnp.bfloat16)


def analysed(perturb, state_mean, routed):
    return pl.pallas_call(
        analysis_kernel,
        out_shape=jax.ShapeDtypeStruct(
            (PATCH_REG, MEMBERS, perturb.shape[2]), jnp.bfloat16
        ),
        compiler_params=pltpu.CompilerParams(vmem_limit_bytes=12 << 20),
        name="analysed",
    )(perturb, state_mean, *routed)


def swap(x, bit):
    return lax.ppermute(x, "mem", [(j, j ^ bit) for j in range(4)])


def to_owner(x, bit):
    axes = ("mem", "ylo", "zq", "zp")
    sizes = [lax.axis_size(a) for a in axes]
    pairs = []
    for m, y, z, h in itertools.product(*(range(n) for n in sizes)):
        goal = (m ^ bit, (y + 1) % sizes[1], (z + ALONG[m]) % sizes[2], sizes[3] - 1 - h if m == 1 else h)
        flat = [((a * sizes[1] + b) * sizes[2] + c) * sizes[3] + d for a, b, c, d in ((m, y, z, h), goal)]
        pairs.append(tuple(flat))
    return lax.ppermute(x, axes, pairs)


def per_device(prior, anomalies, spread, departure, tally, zone, tile):
    ways = {a: lax.axis_size(a) for a in ("ylo", "x", "zq", "zp")}
    in_hbm = lambda x: pltpu.with_memory_space_constraint(x, pltpu.HBM)
    far = swap(prior.reshape(-1, prior.shape[2]), 2)
    messages = build_messages(
        *(in_hbm(x) for x in (anomalies, spread, departure, tally, tile, zone[:, 0])),
        tuple(ways.values()),
    )
    arrived = lax.all_to_all(messages, GROUP, split_axis=0, concat_axis=0, tiled=True)
    arrived, prior = lax.optimization_barrier((arrived, prior))
    near = swap(prior, 1)

    pieces = partial_grams(arrived)
    same, other = to_owner(pieces[0], 0), to_owner(pieces[1], 2)

    farther = swap(far, 1)
    far, farther = (x.reshape(prior.shape) for x in (far, farther))
    field = jnp.concatenate([prior, near, far, farther], axis=0).transpose(1, 0, 2)
    state_mean = jnp.sum(field, axis=1, keepdims=True, dtype=jnp.float32) / SAMPLE_NUMBER
    perturb = (field - state_mean).astype(jnp.bfloat16)
    other, state_mean, perturb = lax.optimization_barrier((other, state_mean, perturb))
    crossed = [swap(x[1], 1) for x in (same, other)]
    weights = flipped_weights((same, other, *crossed))
    routed = [weights[0]] + [swap(weights[e], e) for e in range(1, 4)]
    return analysed(perturb, state_mean, routed).transpose(1, 0, 2)


def solution(mesh):
    grid = Mesh(mesh.devices.reshape(4, 2, 4, 4, 2), ("mem", "ylo", "x", "zq", "zp"))
    return on_grid(grid)


def on_grid(grid):
    reg = ("ylo", "x", "zq", "zp")
    every = ("mem",) + reg
    placed = (
        P("mem", reg, None),
        P(every, None, None),
        P(every, None),
        P(every, None),
        P(every),
        P(every, None),
        P(every),
    )
    return jax.shard_map(
        per_device, mesh=grid, in_specs=placed, out_specs=P("mem", reg, None), check_vma=False
    )
```
